32 devices in a mesh: row: 4 (over y, core), col: 8 (over z, x).
Axes of the slice: x: 2, y: 2, z: 4, core: 2. Of those that a mesh axis runs over, the one named last changes fastest.
Arguments:
- tokens: bfloat16 [3072, 6144], P('row'), may hold values from -6 to 6
- routes: int32 [3072, 2], P('row'), may hold values from 0 to 7, as said below
- w_master: float32 [6144, 2, 9216], P('row', None, 'col'), may hold values from -1 to 1
- d_hidden: bfloat16 [768, 9216], P('row', 'col'), may hold values from -6 to 6
Outputs:
- hidden: bfloat16 [768, 9216], P('row', 'col')
- update: float32 [6144, 2, 9216], P('row', None, 'col')
- new_master: float32 [6144, 2, 9216], P('row', None, 'col')
The draws below stay inside these ranges and needn't reach their ends.
Inputs may be any that keep to these rules, and one draw needn't show every extreme that they name: `routes`: in every aligned block of 768 tokens exactly 192 tokens name expert 0; the two experts of a token differ; every expert is named.
All inputs are finite; a program needn't handle non-finite values. Where the reference program divides by a largest or mean magnitude, that divisor is 1e-20 or more.
Results may differ from the reference program's by a relative error of at most 0.023.
Values may be sent and summed in bfloat16 or wider, within the bound.
A program may use at most 128 MiB of HBM per device.

```python
import jax
import jax.numpy as jnp
from jax import lax

D = 6144
EXPERTS = 8
FFW = 9216
BLK = 128
TOK_ROW = 768
CAP = 192
TOKENS = 3072
SLOTS = 768
N_ROW = 4


def draw_routes(key, part):
    blocks = TOKENS // TOK_ROW
    keys = jax.random.split(jax.random.fold_in(key, 11), 4)
    orders = jax.vmap(lambda k: jax.random.permutation(k, TOK_ROW))(jax.random.split(keys[0], blocks))
    chosen = orders < CAP
    first = jax.random.randint(keys[1], (blocks, TOK_ROW), 1, EXPERTS)
    offset = jax.random.randint(keys[2], (blocks, TOK_ROW), 1, EXPERTS - 1)
    second = (first - 1 + offset) % (EXPERTS - 1) + 1
    flipped = jax.random.randint(keys[3], (blocks, TOK_ROW), 0, 2)
    leading = jnp.where(chosen, 0, first)
    column_one = jnp.where(flipped == 1, second, leading)
    column_two = jnp.where(flipped == 1, leading, second)
    return jnp.stack([column_one, column_two], axis=-1).reshape(TOKENS, 2).astype(jnp.int32)


def draw_w_master(key, part):
    keys = jax.random.split(jax.random.fold_in(key, 23), 3)
    row_bands = jnp.exp(jax.random.uniform(keys[0], (D // BLK,), jnp.float32, 0.0, jnp.log(10.0)))
    row_scale = jnp.repeat(row_bands, BLK)
    col_bands = jnp.exp(jax.random.uniform(keys[1], (2, FFW // 32), jnp.float32, jnp.log(0.3), jnp.log(3.0)))
    col_scale = jnp.repeat(col_bands, 32, axis=1)
    base = jnp.clip(jax.random.normal(keys[2], (D, 2, FFW), jnp.float32), -6.0, 6.0)
    values = base * row_scale[:, None, None] * col_scale[None, :, :] / jnp.sqrt(21.5 * D)
    return values.astype(jnp.float32)


def block_scale(rng, shape, cuts, least, high):
    loudness, own = 1.0, jax.random.fold_in(rng, 6)
    for dim, parts in cuts:
        draws = jnp.exp(jax.random.uniform(jax.random.fold_in(own, dim), (parts,), jnp.float32, least / len(cuts), high / len(cuts)))
        loudness = loudness * jnp.repeat(draws, shape[dim] // parts).reshape([-1 if axis == dim else 1 for axis in range(len(shape))])
    return loudness


def gaussian(key, shape, deviation, most, pieces=(), held_as=jnp.bfloat16):
    drawn = deviation * jax.random.normal(key, shape, jnp.float32)
    if pieces:
        drawn = drawn * block_scale(key, shape, pieces, -0.22, 0.18)
    return jnp.clip(drawn, -most, most).astype(held_as)


def setup_inputs(seed: int = 0) -> dict:
    streams_of = jax.random.split(jax.random.key(seed), 5)
    tokens = gaussian(streams_of[0], (TOKENS, D), 1.0, 6.0, ((0, 4),))
    routes = draw_routes(jax.random.fold_in(streams_of[4], 71), 0)
    w_master = draw_w_master(jax.random.fold_in(streams_of[4], 71), 0)
    d_hidden = gaussian(streams_of[3], (SLOTS, FFW), 1.0, 6.0, ((0, 4), (1, 8)))
    return {"tokens": tokens, "routes": routes, "w_master": w_master, "d_hidden": d_hidden}


epsilon = 1e-6
quant_range = 448.0
learn_rate = 0.05


def reference(tokens, routes, w_master, d_hidden):
    colmax = jnp.max(jnp.abs(w_master), axis=0)
    wscale = (colmax + epsilon) / quant_range
    quantized = (w_master / wscale).astype(jnp.bfloat16)
    routed = jnp.any(routes == 0, axis=1).reshape(N_ROW, TOK_ROW)

    def choose(flags):
        return jnp.nonzero(flags, size=CAP)[0].astype(jnp.int32)

    positions = jax.vmap(choose)(routed) + (jnp.arange(N_ROW, dtype=jnp.int32) * TOK_ROW)[:, None]
    slot_rows = tokens[positions.reshape(-1)]
    group_width = D // N_ROW
    weight_groups = quantized.reshape(N_ROW, group_width, 2 * FFW)
    row_slices = jnp.transpose(slot_rows.reshape(SLOTS, N_ROW, group_width), (1, 0, 2))

    def add_rows(carry_sum, items):
        slot_part, weight_part = items
        term = jnp.dot(slot_part, weight_part, preferred_element_type=jnp.float32)
        rounded = lax.optimization_barrier(term.astype(jnp.bfloat16)).astype(jnp.float32)
        return carry_sum + rounded, None

    summed, _ = lax.scan(add_rows, jnp.zeros((SLOTS, 2 * FFW), jnp.float32), (row_slices, weight_groups))
    projected = summed.reshape(SLOTS, 2, FFW) * wscale
    gate_pre = projected[:, 0]
    up_pre = projected[:, 1]
    gate_sig = jax.nn.sigmoid(gate_pre)
    gate_act = gate_pre * gate_sig
    hidden = (gate_act * up_pre).astype(jnp.bfloat16)
    upstream = d_hidden.astype(jnp.float32)
    grad_gate = upstream * up_pre * gate_sig * (1.0 + gate_pre * (1.0 - gate_sig))
    grad_up = upstream * gate_act
    grad_pre = jnp.stack([grad_gate, grad_up], axis=1).astype(jnp.bfloat16).reshape(N_ROW, CAP, 2 * FFW)
    group_rows = slot_rows.reshape(N_ROW, CAP, D)

    def add_group(carry_sum, items):
        rows_part, grads_part = items
        block_term = lax.dot_general(rows_part, grads_part, (((0,), (0,)), ((), ())), preferred_element_type=jnp.float32)
        rounded = lax.optimization_barrier(block_term.astype(jnp.bfloat16)).astype(jnp.float32)
        return carry_sum + rounded, None

    grad_full, _ = lax.scan(add_group, jnp.zeros((D, 2 * FFW), jnp.float32), (group_rows, grad_pre))
    grad_full = grad_full.reshape(D // BLK, BLK, 2, FFW)
    block_max = jnp.max(jnp.abs(grad_full), axis=(1, 3))
    update = (grad_full / (block_max[:, None, :, None] + epsilon)).reshape(D, 2, FFW)
    new_master = w_master - learn_rate * colmax * update
    return hidden, update, new_master
```

```python
import jax
import jax.numpy as jnp
from jax import lax
from jax.experimental import pallas as pl
from jax.experimental.pallas import tpu as pltpu
from jax.sharding import PartitionSpec as P

BLK = 128


epsilon = 1e-06
quant_range = 448.0
learn_rate = 0.05


def on_device_plain(tokens, routes, w_master, d_hidden):
    rows_local, _, columns = w_master.shape
    slots = d_hidden.shape[0]
    colmax = lax.pmax(jnp.max(jnp.abs(w_master), axis=0), "row")
    wscale = (colmax + epsilon) / quant_range
    quantized = (w_master / wscale).astype(jnp.bfloat16).reshape(rows_local, 2 * columns)
    flat_scale = wscale.reshape(2 * columns)
    routed = jnp.any(routes == 0, axis=1)
    picked = jnp.nonzero(routed, size=slots)[0].astype(jnp.int32)
    slot_rows = tokens[picked]
    slot_cols = lax.all_to_all(slot_rows, "row", split_axis=1, concat_axis=0, tiled=True)
    slot_part = lax.slice_in_dim(slot_cols, 0, lax.axis_size("row") * slots, axis=0)
    summed = lax.psum_scatter(
        jnp.dot(slot_part, quantized, preferred_element_type=jnp.float32).astype(jnp.bfloat16),
        "row",
        scatter_dimension=0,
        tiled=True,
    ).astype(jnp.float32)
    projected = (summed * flat_scale).reshape(slots, 2, columns)
    gate_pre = projected[:, 0]
    up_pre = projected[:, 1]
    gate_sig = jax.nn.sigmoid(gate_pre)
    gate_act = gate_pre * gate_sig
    hidden = (gate_act * up_pre).astype(jnp.bfloat16)
    upstream = d_hidden.astype(jnp.float32)
    grad_gate = upstream * up_pre * gate_sig * (1.0 + gate_pre * (1.0 - gate_sig))
    grad_up = upstream * gate_act
    grad_pre = (
        jnp.stack([grad_gate, grad_up], axis=1).astype(jnp.bfloat16).reshape(slots, 2 * columns)
    )
    shard_piece = lax.all_gather(grad_pre, "row", axis=0, tiled=True)
    groups = shard_piece.shape[0] // slots
    slot_part = lax.slice_in_dim(slot_cols, 0, shard_piece.shape[0], axis=0).reshape(
        groups, slots, rows_local
    )
    block_terms = jnp.einsum(
        "gsd,gsf->gdf",
        slot_part,
        shard_piece.reshape(groups, slots, 2 * columns),
        preferred_element_type=jnp.float32,
    )
    rounded = lax.optimization_barrier(block_terms.astype(jnp.bfloat16)).astype(jnp.float32)
    grad_full = jnp.sum(rounded, axis=0)
    grad_blocks = grad_full.reshape(rows_local // BLK, BLK, 2, columns)
    block_max = lax.pmax(jnp.max(jnp.abs(grad_blocks), axis=(1, 3)), "col")
    update = (grad_blocks / (block_max[:, None, :, None] + epsilon)).reshape(rows_local, 2, columns)
    new_master = w_master - learn_rate * colmax * update
    return (hidden, update, new_master)


LANE = 128
SUB = 8
LEAD = 3


def moved(src, dst, send, recv, to):
    return pltpu.make_async_remote_copy(
        src_ref=src,
        dst_ref=dst,
        send_sem=send,
        recv_sem=recv,
        device_id=to,
        device_id_type=pl.DeviceIdType.MESH,
    )


def flipped(index, bit):
    return index + bit - 2 * bit * lax.rem(index // bit, 2)


def layer_kernel(
    routes_hbm, dh_hbm, tok_hbm, w_hbm, hid, grad_ref, cm_ref, inv_ref, wv,
    routes, dh, tokv, tokq, psendt, qsend, sc, turned, folded, cmx,
    psend, prec, keep, own, xsend, xrec, ga, tops, bmx,
    in_sem, tok_sem, w_sem, pt_send, pt_recv, y_send, y_recv, x_send, x_recv, z_send, z_recv,
    c_send, c_recv, b_send, b_recv,
    p_send, p_recv, xs_send, xs_recv, ga_send, ga_recv, gp_send, gp_recv, gf_send, gf_recv,
):
    me = lax.axis_index("row")
    col = lax.axis_index("col")
    core = lax.rem(me, 2)
    partner = me + 1 - 2 * core
    across = lax.rem(me + 2, 4)
    diag = lax.rem(partner + 2, 4)
    where_to = (me, across, partner, diag)
    group = bmx.shape[0]
    col_x = flipped(col, 1)
    col_z = flipped(col, 2)
    col_far = flipped(col, 4)
    quarter_of = lax.rem(col, 4)
    quarter_x = lax.rem(col_x, 4)
    quarter_z = lax.rem(col_z, 4)
    tiles = ga.shape[0]
    slots = hid.shape[0]
    rows = sc.shape[1]
    toks = routes.shape[1]
    chunks = w_sem.shape[1]
    piece = rows // chunks
    quarter = rows // 4
    half = slots // 2

    in_copies = (
        pltpu.make_async_copy(routes_hbm, routes, in_sem.at[0]),
        pltpu.make_async_copy(dh_hbm, dh, in_sem.at[1]),
    )
    in_copies[0].start()
    q_copies = {}
    for n, j in enumerate((1, 3)):
        cols = pl.ds(pl.multiple_of(where_to[j] * rows + quarter_of * quarter, LANE), quarter)
        q_copies[n] = pltpu.make_async_copy(tok_hbm.at[:, cols], tokq.at[n], tok_sem.at[n])
        q_copies[n].start()
    tok_copies = {}
    for n, j in enumerate((2, 0)):
        cols = pl.ds(pl.multiple_of(where_to[j] * rows, LANE), rows)
        tok_copies[n] = pltpu.make_async_copy(tok_hbm.at[:, cols], tokv.at[n], tok_sem.at[2 + n])
        tok_copies[n].start()
    w_copies = []
    for k in range(chunks):
        part = pl.ds(k * piece, piece)
        for p in range(2):
            w_copies.append(
                pltpu.make_async_copy(w_hbm.at[part, p, :], wv.at[p, part], w_sem.at[p, k])
            )
            w_copies[-1].start()
    in_copies[1].start()

    barrier = pltpu.get_barrier_semaphore()
    greeted = [{"row": where_to[j]} for j in (1, 2, 3)] + [{"col": c} for c in (col_x, col_z, col_far)]
    for device in greeted:
        pl.semaphore_signal(barrier, inc=1, device_id=device, device_id_type=pl.DeviceIdType.MESH)

    before = lax.broadcasted_iota(jnp.int32, (LANE, LANE), 0)
    after = lax.broadcasted_iota(jnp.int32, (LANE, LANE), 1)
    ladder = jnp.where(before < after, 1.0, 0.0).astype(jnp.bfloat16)
    every = jnp.ones((LANE, LANE), jnp.bfloat16)
    in_copies[0].wait()
    named = jnp.logical_or(routes[0:1, :] == 0, routes[1:2, :] == 0)
    flag = jnp.where(named, 1.0, 0.0)
    mask = jnp.broadcast_to(flag, (16, toks)).astype(jnp.bfloat16)
    earlier = jnp.zeros((16, LANE), jnp.float32)
    places = []
    for k in range(toks // LANE):
        part = mask[:, k * LANE : (k + 1) * LANE]
        places.append(earlier + jnp.dot(part, ladder, preferred_element_type=jnp.float32))
        earlier = earlier + jnp.dot(part, every, preferred_element_type=jnp.float32)
    place = jnp.concatenate(places, axis=1)[0:1, :].astype(jnp.int32)
    slot_id = lax.broadcasted_iota(jnp.int32, (slots, toks), 0)
    pick = jnp.where(slot_id == place, flag, 0.0).astype(jnp.bfloat16)
    pl.semaphore_wait(barrier, len(greeted))

    def routed(c, q):
        j = (1, 3)[c // 2]
        return sc.at[
            pl.ds(j * slots + (c % 2) * half, half),
            pl.ds(pl.multiple_of(q * quarter, LANE), quarter),
        ]

    y_copies = []
    for c in range(4):
        n = c // 2
        if c % 2 == 0:
            q_copies[n].wait()
            qsend[n] = jnp.dot(pick, tokq[n], preferred_element_type=jnp.float32).astype(jnp.bfloat16)
        y_copies.append(
            moved(
                qsend.at[n, pl.ds((c % 2) * half, half)],
                routed(c, quarter_of),
                y_send.at[c],
                y_recv.at[c],
                {"row": where_to[(1, 3)[n]]},
            )
        )
        y_copies[-1].start()
    tok_copies[0].wait()
    psendt[...] = jnp.dot(pick, tokv[0], preferred_element_type=jnp.float32).astype(jnp.bfloat16)
    t_copy = moved(psendt, sc.at[pl.ds(2 * slots, slots)], pt_send.at[0], pt_recv.at[0], {"row": partner})
    t_copy.start()
    tok_copies[1].wait()
    sc[0:slots, :] = jnp.dot(pick, tokv[1], preferred_element_type=jnp.float32).astype(jnp.bfloat16)

    x_copies = [moved(routed(c, quarter_of), routed(c, quarter_of), x_send.at[c], x_recv.at[c], {"col": col_x}) for c in range(4)]
    z_copies = [moved(routed(c, quarter_of), routed(c, quarter_of), z_send.at[c], z_recv.at[c], {"col": col_z}) for c in range(4)]
    for n in range(2):
        x_copies.append(
            moved(routed(2 * n + 1, quarter_z), routed(2 * n + 1, quarter_z), x_send.at[4 + n], x_recv.at[4 + n], {"col": col_x})
        )
        z_copies.append(
            moved(routed(2 * n, quarter_x), routed(2 * n, quarter_x), z_send.at[4 + n], z_recv.at[4 + n], {"col": col_z})
        )

    def pass_on(c):
        y_copies[c].wait_recv()
        x_copies[c].start()
        z_copies[c].start()

    def pass_x(n):
        x_copies[2 * n].wait_recv()
        z_copies[4 + n].start()

    def pass_z(n):
        z_copies[2 * n + 1].wait_recv()
        x_copies[4 + n].start()

    folded[...] = jnp.zeros(folded.shape, jnp.float32)

    def fold_chunk(k):
        for p in range(2):
            w_copies[2 * k + p].wait()

        def fold(t, carry):
            cols = pl.ds(pl.multiple_of(t * LANE, LANE), LANE)
            for p in range(2):
                tile = jnp.abs(wv[p, k * piece : (k + 1) * piece, cols])
                best = jnp.max(tile.reshape(-1, SUB, LANE), axis=0)
                folded[p, :, cols] = jnp.maximum(folded[p, :, cols], best)
            return carry

        lax.fori_loop(0, tiles, fold, 0)

    order = (
        lambda: pass_on(0), lambda: pass_on(1), lambda: pass_on(2),
        lambda: pass_x(0), lambda: pass_z(0), lambda: pass_on(3),
    )
    for k in range(chunks):
        fold_chunk(k)
        if k < len(order):
            order[k]()
    for p in range(2):
        cmx[0, p : p + 1, :] = jnp.max(folded[p], axis=0, keepdims=True)
    c_copies = []
    for j in (1, 2, 3):
        c_copies.append(
            moved(cmx.at[0], cmx.at[j], c_send.at[j - 1], c_recv.at[j - 1], {"row": where_to[j]})
        )
        c_copies[-1].start()
    turned[:, 0:slots] = sc[0:slots, :].T
    t_copy.wait()
    turned[:, 2 * slots : 3 * slots] = sc[2 * slots : 3 * slots, :].T
    pass_x(1)
    pass_z(1)
    for copy in c_copies:
        copy.wait()
    cm_ref[...] = jnp.maximum(jnp.maximum(cmx[0], cmx[1]), jnp.maximum(cmx[2], cmx[3]))
    tops[...] = jnp.zeros(tops.shape, jnp.float32)
    in_copies[1].wait()
    for c in range(4):
        y_copies[c].wait_send()
    for copies, late in ((x_copies, (1, 3, 4, 5)), (z_copies, (0, 2, 4, 5))):
        for c in late:
            copies[c].wait_recv()

    def scale_row(t, p):
        cols = pl.ds(pl.multiple_of(t * LANE, LANE), LANE)
        return (cm_ref[p : p + 1, cols] + epsilon) / quant_range

    def swap(t):
        return moved(psend.at[t], prec.at[t], p_send.at[t], p_recv.at[t], {"row": partner})

    def cross(t):
        return moved(xsend.at[t], xrec.at[t], xs_send.at[t], xs_recv.at[t], {"row": across})

    def grad_block(t, j):
        return ga.at[t, pl.ds(j * slots, slots)]

    def share_across(t):
        return moved(grad_block(t, 0), grad_block(t, 1), ga_send.at[t], ga_recv.at[t], {"row": across})

    def share_partner(t):
        return moved(grad_block(t, 0), grad_block(t, 2), gp_send.at[t], gp_recv.at[t], {"row": partner})

    def forward(t):
        return moved(grad_block(t, 1), grad_block(t, 3), gf_send.at[t], gf_recv.at[t], {"row": partner})

    depth = 3 * BLK

    def step(i, carry):
        @pl.when(i < tiles)
        def _():
            t = i
            halves = []
            for p in range(2):
                w = wv[p, :, pl.ds(pl.multiple_of(t * LANE, LANE), LANE)]
                halves.append((w * (1.0 / scale_row(t, p))).astype(jnp.bfloat16))
            quantized = jnp.concatenate(halves, axis=1)
            term = jnp.dot(sc[...], quantized, preferred_element_type=jnp.float32)
            slot = lax.rem(t, 2)
            psend[t] = term[2 * slots :].astype(jnp.bfloat16)
            keep[slot] = term[: 2 * slots]
            swap(t).start()

        @pl.when(jnp.logical_and(i >= 1, i < tiles + 1))
        def _():
            t = i - 1
            slot = lax.rem(t, 2)
            swap(t).wait_recv()
            own[t] = keep[slot, :slots] + prec[t, :slots].astype(jnp.float32)
            xsend[t] = (keep[slot, slots:] + prec[t, slots:].astype(jnp.float32)).astype(jnp.bfloat16)
            cross(t).start()

        @pl.when(i == 1)
        def _():
            for j in (1, 3):
                turned[:, j * slots : (j + 1) * slots] = sc[j * slots : (j + 1) * slots, :].T

        @pl.when(jnp.logical_and(i >= 1 + LEAD, i < tiles + 1 + LEAD))
        def _():
            t = i - 1 - LEAD
            cross(t).wait_recv()
            total = own[t] + xrec[t].astype(jnp.float32)
            gate_pre = total[:, :LANE] * scale_row(t, 0)
            up_pre = total[:, LANE:] * scale_row(t, 1)
            gate_sig = jax.nn.sigmoid(gate_pre)
            gate_act = gate_pre * gate_sig
            cols = pl.ds(pl.multiple_of(t * LANE, LANE), LANE)
            hid[:, cols] = (gate_act * up_pre).astype(jnp.bfloat16)
            upstream = dh[:, cols].astype(jnp.float32)
            grad_gate = upstream * up_pre * gate_sig * (1.0 + gate_pre * (1.0 - gate_sig))
            grad_up = upstream * gate_act
            ga[t, 0:slots, :] = jnp.concatenate([grad_gate, grad_up], axis=1).astype(jnp.bfloat16)
            share_across(t).start()
            share_partner(t).start()

        @pl.when(jnp.logical_and(i >= 3 + LEAD, i < tiles + 3 + LEAD))
        def _():
            t = i - 3 - LEAD
            share_across(t).wait_recv()
            forward(t).start()

        @pl.when(i >= 4 + LEAD)
        def _():
            t = i - 4 - LEAD
            share_partner(t).wait_recv()
            forward(t).wait_recv()
            cols = pl.ds(pl.multiple_of(t * 2 * LANE, 2 * LANE), 2 * LANE)
            for k in range(rows // depth):
                grad = jnp.dot(turned[k * depth : (k + 1) * depth, :], ga[t], preferred_element_type=jnp.float32)
                grad_ref[k * depth : (k + 1) * depth, cols] = grad.astype(jnp.bfloat16)
                for b in range(3):
                    for p in range(2):
                        n = 2 * (3 * k + b) + p
                        tile = jnp.abs(grad[b * BLK : (b + 1) * BLK, p * LANE : (p + 1) * LANE])
                        tops[n] = jnp.maximum(tops[n], jnp.max(tile.reshape(-1, SUB, LANE), axis=0))

        return carry

    lax.fori_loop(0, tiles + 4 + LEAD, step, 0)

    for n in range(tops.shape[0]):
        bmx[0, n : n + 1, :] = jnp.max(tops[n], axis=0, keepdims=True)
    b_copies = []
    for k in range(1, group):
        b_copies.append(
            moved(bmx.at[0], bmx.at[k], b_send.at[k - 1], b_recv.at[k - 1], {"col": lax.rem(col + k, group)})
        )
        b_copies[-1].start()

    def finish(t, carry):
        swap(t).wait_send()
        cross(t).wait_send()
        share_across(t).wait_send()
        share_partner(t).wait_send()
        forward(t).wait_send()
        return carry

    lax.fori_loop(0, tiles, finish, 0)
    for copies in (x_copies, z_copies):
        for copy in copies:
            copy.wait_send()
    for copy in b_copies:
        copy.wait()
    best = bmx[0]
    for k in range(1, group):
        best = jnp.maximum(best, bmx[k])
    block_max = jnp.max(best, axis=1, keepdims=True)
    inv_ref[...] = jnp.broadcast_to(1.0 / (block_max + epsilon), inv_ref.shape)


def update_kernel(inv_ref, cm_ref, grad_ref, hid, wv, out_hbm, update_hbm, new_hbm, uv, nv, u_sem, n_sem, h_sem):
    blocks = u_sem.shape[1]
    columns = wv.shape[2]
    tiles = columns // LANE

    def part(b):
        return pl.ds(pl.multiple_of(b * BLK, BLK), BLK)

    def put_update(b, p):
        return pltpu.make_async_copy(uv.at[p, part(b)], update_hbm.at[part(b), p, :], u_sem.at[p, b])

    def put_new(b, p):
        return pltpu.make_async_copy(nv.at[p, part(b)], new_hbm.at[part(b), p, :], n_sem.at[p, b])

    def step(b, carry):
        for p in range(2):
            inverse = inv_ref[pl.ds(2 * b + p, 1), :]
            for t in range(tiles):
                cols = slice(t * LANE, (t + 1) * LANE)
                at = (2 * t + p) * LANE
                update = grad_ref[part(b), at : at + LANE].astype(jnp.float32) * inverse
                uv[p, part(b), cols] = update
                nv[p, part(b), cols] = wv[p, part(b), cols] - (learn_rate * cm_ref[p : p + 1, cols]) * update
            put_update(b, p).start()
            put_new(b, p).start()
        return carry

    def finish(b, carry):
        for p in range(2):
            put_update(b, p).wait()
            put_new(b, p).wait()
        return carry

    put_hidden = pltpu.make_async_copy(hid, out_hbm, h_sem.at[0])
    put_hidden.start()
    lax.fori_loop(0, blocks, step, 0)
    lax.fori_loop(0, blocks, finish, 0)
    put_hidden.wait()


def on_device(tokens, routes, w_master, d_hidden):
    rows, _, columns = w_master.shape
    slots = d_hidden.shape[0]
    toks = tokens.shape[0]
    aligned = columns % LANE == 0 and rows % (12 * BLK) == 0 and slots % 32 == 0 and toks % LANE == 0
    if lax.axis_size("row") != 4 or lax.axis_size("col") != 8 or not aligned:
        return on_device_plain(tokens, routes, w_master, d_hidden)
    group = lax.axis_size("col")
    tiles = columns // LANE
    bf16, f32 = jnp.bfloat16, jnp.float32
    chunks = 6
    blocks = rows // BLK
    vmem = pl.BlockSpec(memory_space=pltpu.VMEM)
    hbm = pl.BlockSpec(memory_space=pltpu.HBM)
    dma = pltpu.SemaphoreType.DMA
    wide = 2 * LANE
    hidden, grad, colmax, inverse, master = pl.pallas_call(
        layer_kernel,
        name="layer_exchange",
        out_shape=(
            jax.ShapeDtypeStruct((slots, columns), bf16),
            pltpu.VMEM((rows, 2 * columns), bf16),
            jax.ShapeDtypeStruct((2, columns), f32),
            jax.ShapeDtypeStruct((2 * blocks, LANE), f32),
            pltpu.VMEM((2, rows, columns), f32),
        ),
        in_specs=[hbm, hbm, hbm, hbm],
        out_specs=(vmem,) * 5,
        scratch_shapes=[
            pltpu.VMEM((2, toks), jnp.int32),
            pltpu.VMEM((slots, columns), bf16),
            pltpu.VMEM((2, toks, rows), bf16),
            pltpu.VMEM((2, toks, rows // 4), bf16),
            pltpu.VMEM((slots, rows), bf16),
            pltpu.VMEM((2, slots, rows // 4), bf16),
            pltpu.VMEM((4 * slots, rows), bf16),
            pltpu.VMEM((rows, 4 * slots), bf16),
            pltpu.VMEM((2, SUB, columns), f32),
            pltpu.VMEM((4, 2, columns), f32),
            pltpu.VMEM((tiles, 2 * slots, wide), bf16),
            pltpu.VMEM((tiles, 2 * slots, wide), bf16),
            pltpu.VMEM((2, 2 * slots, wide), f32),
            pltpu.VMEM((tiles, slots, wide), f32),
            pltpu.VMEM((tiles, slots, wide), bf16),
            pltpu.VMEM((tiles, slots, wide), bf16),
            pltpu.VMEM((tiles, 4 * slots, wide), bf16),
            pltpu.VMEM((2 * blocks, SUB, LANE), f32),
            pltpu.VMEM((group, 2 * blocks, LANE), f32),
            dma((2,)),
            dma((4,)),
            dma((2, chunks)),
            dma((1,)),
            dma((1,)),
            dma((4,)),
            dma((4,)),
            dma((6,)),
            dma((6,)),
            dma((6,)),
            dma((6,)),
            dma((3,)),
            dma((3,)),
            dma((group - 1,)),
            dma((group - 1,)),
        ]
        + [dma((tiles,))] * 10,
        compiler_params=pltpu.CompilerParams(
            collective_id=0, has_side_effects=True, vmem_limit_bytes=26 * 1024 * 1024
        ),
    )(*(pltpu.with_memory_space_constraint(x, pltpu.HBM) for x in (routes.T, d_hidden, tokens, w_master)))
    hidden, update, new_master = pl.pallas_call(
        update_kernel,
        name="master_update",
        out_shape=(jax.ShapeDtypeStruct((slots, columns), bf16),)
        + (jax.ShapeDtypeStruct(w_master.shape, f32),) * 2,
        in_specs=[vmem] * 5,
        out_specs=(hbm, hbm, hbm),
        scratch_shapes=[
            pltpu.VMEM((2, rows, columns), f32),
            pltpu.VMEM((2, rows, columns), f32),
            dma((2, blocks)),
            dma((2, blocks)),
            dma((1,)),
        ],
        compiler_params=pltpu.CompilerParams(vmem_limit_bytes=30 * 1024 * 1024),
    )(inverse, colmax, grad, hidden, master)
    return (hidden, update, new_master)


def solution(mesh):
    in_specs = (P("row", None), P("row", None), P("row", None, "col"), P("row", "col"))
    out_specs = (P("row", "col"), P("row", None, "col"), P("row", None, "col"))
    return jax.shard_map(
        on_device, mesh=mesh, in_specs=in_specs, out_specs=out_specs, check_vma=False
    )
```

```python
import jax
import jax.numpy as jnp
from jax import lax
from jax.experimental import pallas as pl
from jax.experimental.pallas import tpu as pltpu
from jax.sharding import PartitionSpec as P

BLK = 128


epsilon = 1e-06
quant_range = 448.0
learn_rate = 0.05


def on_device_plain(tokens, routes, w_master, d_hidden):
    rows_local, _, columns = w_master.shape
    slots = d_hidden.shape[0]
    colmax = lax.pmax(jnp.max(jnp.abs(w_master), axis=0), "row")
    wscale = (colmax + epsilon) / quant_range
    quantized = (w_master / wscale).astype(jnp.bfloat16).reshape(rows_local, 2 * columns)
    flat_scale = wscale.reshape(2 * columns)
    routed = jnp.any(routes == 0, axis=1)
    picked = jnp.nonzero(routed, size=slots)[0].astype(jnp.int32)
    slot_rows = tokens[picked]
    slot_cols = lax.all_to_all(slot_rows, "row", split_axis=1, concat_axis=0, tiled=True)
    slot_part = lax.slice_in_dim(slot_cols, 0, lax.axis_size("row") * slots, axis=0)
    summed = lax.psum_scatter(
        jnp.dot(slot_part, quantized, preferred_element_type=jnp.float32).astype(jnp.bfloat16),
        "row",
        scatter_dimension=0,
        tiled=True,
    ).astype(jnp.float32)
    projected = (summed * flat_scale).reshape(slots, 2, columns)
    gate_pre = projected[:, 0]
    up_pre = projected[:, 1]
    gate_sig = jax.nn.sigmoid(gate_pre)
    gate_act = gate_pre * gate_sig
    hidden = (gate_act * up_pre).astype(jnp.bfloat16)
    upstream = d_hidden.astype(jnp.float32)
    grad_gate = upstream * up_pre * gate_sig * (1.0 + gate_pre * (1.0 - gate_sig))
    grad_up = upstream * gate_act
    grad_pre = (
        jnp.stack([grad_gate, grad_up], axis=1).astype(jnp.bfloat16).reshape(slots, 2 * columns)
    )
    shard_piece = lax.all_gather(grad_pre, "row", axis=0, tiled=True)
    groups = shard_piece.shape[0] // slots
    slot_part = lax.slice_in_dim(slot_cols, 0, shard_piece.shape[0], axis=0).reshape(
        groups, slots, rows_local
    )
    block_terms = jnp.einsum(
        "gsd,gsf->gdf",
        slot_part,
        shard_piece.reshape(groups, slots, 2 * columns),
        preferred_element_type=jnp.float32,
    )
    rounded = lax.optimization_barrier(block_terms.astype(jnp.bfloat16)).astype(jnp.float32)
    grad_full = jnp.sum(rounded, axis=0)
    grad_blocks = grad_full.reshape(rows_local // BLK, BLK, 2, columns)
    block_max = lax.pmax(jnp.max(jnp.abs(grad_blocks), axis=(1, 3)), "col")
    update = (grad_blocks / (block_max[:, None, :, None] + epsilon)).reshape(rows_local, 2, columns)
    new_master = w_master - learn_rate * colmax * update
    return (hidden, update, new_master)


LANE = 128
SUB = 8
LEAD = 6


def moved(src, dst, send, recv, to):
    return pltpu.make_async_remote_copy(
        src_ref=src,
        dst_ref=dst,
        send_sem=send,
        recv_sem=recv,
        device_id=to,
        device_id_type=pl.DeviceIdType.MESH,
    )


def flipped(index, bit):
    return index + bit - 2 * bit * lax.rem(index // bit, 2)


def layer_kernel(
    routes_hbm, dh_hbm, tok_hbm, w_hbm, hid, grad_ref, cm_ref, inv_ref, wv,
    routes, dh, tokv, tokq, psendt, qsend, sc, turned, folded, cmx, wq,
    esend, erec, own, lsend, lrec, keep, xsend, xrec, ga, tops, bmx,
    in_sem, tok_sem, w_sem, pt_send, pt_recv, y_send, y_recv, x_send, x_recv, z_send, z_recv,
    c_send, c_recv, b_send, b_recv, l_send, l_recv, xs_send, xs_recv,
    e_send, e_recv, ga_send, ga_recv, gp_send, gp_recv, gf_send, gf_recv,
):
    me = lax.axis_index("row")
    col = lax.axis_index("col")
    core = lax.rem(me, 2)
    partner = me + 1 - 2 * core
    across = lax.rem(me + 2, 4)
    diag = lax.rem(partner + 2, 4)
    group = bmx.shape[0]
    col_x = flipped(col, 1)
    col_z = flipped(col, 2)
    col_far = flipped(col, 4)
    quarter_of = lax.rem(col, 4)
    tiles = ga.shape[0]
    slots = hid.shape[0]
    rows = sc.shape[1]
    toks = routes.shape[1]
    chunks = w_sem.shape[1]
    piece = rows // chunks
    quarter = rows // 4
    half = slots // 2

    in_copies = (
        pltpu.make_async_copy(routes_hbm, routes, in_sem.at[0]),
        pltpu.make_async_copy(dh_hbm, dh, in_sem.at[1]),
    )
    in_copies[0].start()
    q_copies = []
    for n in range(4):
        q = (quarter_of, 3 - quarter_of)[n // 2]
        cols = pl.ds(pl.multiple_of((across, diag)[n % 2] * rows + q * quarter, LANE), quarter)
        q_copies.append(pltpu.make_async_copy(tok_hbm.at[:, cols], tokq.at[n], tok_sem.at[n]))
        q_copies[-1].start()
    tok_copies = []
    for n in range(2):
        cols = pl.ds(pl.multiple_of((partner, me)[n] * rows, LANE), rows)
        tok_copies.append(pltpu.make_async_copy(tok_hbm.at[:, cols], tokv.at[n], tok_sem.at[4 + n]))
        tok_copies[-1].start()
    w_copies = []
    for k in range(chunks):
        part = pl.ds(k * piece, piece)
        for p in range(2):
            w_copies.append(
                pltpu.make_async_copy(w_hbm.at[part, p, :], wv.at[p, part], w_sem.at[p, k])
            )
            w_copies[-1].start()
    in_copies[1].start()

    barrier = pltpu.get_barrier_semaphore()
    greeted = [{"row": r} for r in (across, diag, partner)] + [{"col": c} for c in (col_x, col_z, col_far)]
    for device in greeted:
        pl.semaphore_signal(barrier, inc=1, device_id=device, device_id_type=pl.DeviceIdType.MESH)

    before = lax.broadcasted_iota(jnp.int32, (LANE, LANE), 0)
    after = lax.broadcasted_iota(jnp.int32, (LANE, LANE), 1)
    ladder = jnp.where(before < after, 1.0, 0.0).astype(jnp.bfloat16)
    every = jnp.ones((LANE, LANE), jnp.bfloat16)
    in_copies[0].wait()
    named = jnp.logical_or(routes[0:1, :] == 0, routes[1:2, :] == 0)
    flag = jnp.where(named, 1.0, 0.0)
    mask = jnp.broadcast_to(flag, (16, toks)).astype(jnp.bfloat16)
    earlier = jnp.zeros((16, LANE), jnp.float32)
    places = []
    for k in range(toks // LANE):
        part = mask[:, k * LANE : (k + 1) * LANE]
        places.append(earlier + jnp.dot(part, ladder, preferred_element_type=jnp.float32))
        earlier = earlier + jnp.dot(part, every, preferred_element_type=jnp.float32)
    place = jnp.concatenate(places, axis=1)[0:1, :].astype(jnp.int32)
    slot_id = lax.broadcasted_iota(jnp.int32, (slots, toks), 0)
    pick = jnp.where(slot_id == place, flag, 0.0).astype(jnp.bfloat16)
    pl.semaphore_wait(barrier, len(greeted))

    def routed(h, jj, q):
        return sc.at[
            pl.ds((2 + h) * slots + jj * half, half),
            pl.ds(pl.multiple_of(q * quarter, LANE), quarter),
        ]

    def y_copy(h, n):
        return moved(
            qsend.at[n, pl.ds(h * half, half)],
            routed(h, n % 2, (quarter_of, 3 - quarter_of)[n // 2]),
            y_send.at[4 * h + n],
            y_recv.at[4 * h + n],
            {"row": (across, diag)[n % 2]},
        )

    for n in range(4):
        q_copies[n].wait()
        qsend[n] = jnp.dot(pick, tokq[n], preferred_element_type=jnp.float32).astype(jnp.bfloat16)
        y_copy(0, n).start()
    for n in range(4):
        y_copy(1, n).start()
    tok_copies[0].wait()
    psendt[...] = jnp.dot(pick, tokv[0], preferred_element_type=jnp.float32).astype(jnp.bfloat16)
    t_copy = moved(psendt, sc.at[pl.ds(slots, slots)], pt_send.at[0], pt_recv.at[0], {"row": partner})
    t_copy.start()
    tok_copies[1].wait()
    sc[0:slots, :] = jnp.dot(pick, tokv[1], preferred_element_type=jnp.float32).astype(jnp.bfloat16)

    def side_copies(h, jj):
        here = routed(h, jj, quarter_of)
        n = 2 * h + jj
        return (
            moved(here, here, x_send.at[n], x_recv.at[n], {"col": col_x}),
            moved(here, here, z_send.at[n], z_recv.at[n], {"col": col_z}),
        )

    def pass_on(h, jj):
        y_copy(h, jj).wait_recv()
        for copy in side_copies(h, jj):
            copy.start()

    def arrived(h):
        for jj in range(2):
            y_copy(h, 2 + jj).wait_recv()
            for copy in side_copies(h, jj):
                copy.wait_recv()

    folded[...] = jnp.zeros(folded.shape, jnp.float32)

    def fold_chunk(k):
        for p in range(2):
            w_copies[2 * k + p].wait()

        def fold(t, carry):
            cols = pl.ds(pl.multiple_of(t * LANE, LANE), LANE)
            for p in range(2):
                tile = jnp.abs(wv[p, k * piece : (k + 1) * piece, cols])
                best = jnp.max(tile.reshape(-1, SUB, LANE), axis=0)
                folded[p, :, cols] = jnp.maximum(folded[p, :, cols], best)
            return carry

        lax.fori_loop(0, tiles, fold, 0)

    for k in range(chunks):
        fold_chunk(k)
        if k == 2:
            pass_on(0, 0)
        if k == 4:
            pass_on(0, 1)
    for p in range(2):
        cmx[0, p : p + 1, :] = jnp.max(folded[p], axis=0, keepdims=True)
    c_copies = []
    for j, row in enumerate((partner, across, diag)):
        c_copies.append(moved(cmx.at[0], cmx.at[j + 1], c_send.at[j], c_recv.at[j], {"row": row}))
        c_copies[-1].start()
    turned[:, 0:slots] = sc[0:slots, :].T
    t_copy.wait()
    turned[:, slots : 2 * slots] = sc[slots : 2 * slots, :].T
    tops[...] = jnp.zeros(tops.shape, jnp.float32)
    in_copies[1].wait()
    for copy in c_copies:
        copy.wait()
    cm_ref[...] = jnp.maximum(jnp.maximum(cmx[0], cmx[1]), jnp.maximum(cmx[2], cmx[3]))
    arrived(0)

    def scale_row(t, p):
        cols = pl.ds(pl.multiple_of(t * LANE, LANE), LANE)
        return (cm_ref[p : p + 1, cols] + epsilon) / quant_range

    def swap_late(n):
        return moved(lsend.at[n], lrec.at[n], l_send.at[n], l_recv.at[n], {"row": partner})

    def swap_early(t):
        return moved(esend.at[t], erec.at[t], e_send.at[t], e_recv.at[t], {"row": partner})

    def cross(n):
        return moved(xsend.at[n], xrec.at[n], xs_send.at[n], xs_recv.at[n], {"row": across})

    def grad_block(t, j):
        return ga.at[t, pl.ds(j * slots, slots)]

    def share_across(t):
        return moved(grad_block(t, 0), grad_block(t, 2), ga_send.at[t], ga_recv.at[t], {"row": across})

    def share_partner(t):
        return moved(grad_block(t, 0), grad_block(t, 1), gp_send.at[t], gp_recv.at[t], {"row": partner})

    def forward(t):
        return moved(grad_block(t, 2), grad_block(t, 3), gf_send.at[t], gf_recv.at[t], {"row": partner})

    depth = 3 * BLK
    finals = tiles + LEAD

    def step(i, carry):
        @pl.when(i == 1)
        def _():
            pass_on(1, 0)

        @pl.when(i == 2)
        def _():
            pass_on(1, 1)

        @pl.when(i == tiles)
        def _():
            arrived(1)

        @pl.when(i < tiles)
        def _():
            for p in range(2):
                w = wv[p, :, pl.ds(pl.multiple_of(i * LANE, LANE), LANE)]
                wq[i, :, p * LANE : (p + 1) * LANE] = (w * (1.0 / scale_row(i, p))).astype(jnp.bfloat16)

        @pl.when(i < 2 * tiles)
        def _():
            h = i // tiles
            t = lax.rem(i, tiles)
            late = sc[pl.ds(pl.multiple_of((2 + h) * slots, 16), slots), :]
            term = jnp.dot(late, wq[t], preferred_element_type=jnp.float32)
            lsend[i] = term[half:].astype(jnp.bfloat16)
            keep[lax.rem(i, 2)] = term[:half]
            swap_late(i).start()

        @pl.when(jnp.logical_and(i >= 1, i < 2 * tiles + 1))
        def _():
            n = i - 1
            swap_late(n).wait_recv()
            xsend[n] = (keep[lax.rem(n, 2)] + lrec[n].astype(jnp.float32)).astype(jnp.bfloat16)
            cross(n).start()

        @pl.when(jnp.logical_and(i >= tiles, i < 2 * tiles))
        def _():
            t = i - tiles
            term = jnp.dot(sc[0 : 2 * slots, :], wq[t], preferred_element_type=jnp.float32)
            esend[t] = term[slots:].astype(jnp.bfloat16)
            own[t] = term[:slots]
            swap_early(t).start()

        @pl.when(i == tiles + 1)
        def _():
            for jj in range(2):
                block = [sc[(2 + h) * slots + jj * half : (2 + h) * slots + (jj + 1) * half, :] for h in range(2)]
                turned[:, (2 + jj) * slots : (3 + jj) * slots] = jnp.concatenate(block, axis=0).T

        @pl.when(jnp.logical_and(i >= finals, i < finals + tiles))
        def _():
            t = i - finals
            swap_early(t).wait_recv()
            cross(t).wait_recv()
            cross(tiles + t).wait_recv()
            others = jnp.concatenate([xrec[t], xrec[tiles + t]], axis=0).astype(jnp.float32)
            total = own[t] + erec[t].astype(jnp.float32) + others
            gate_pre = total[:, :LANE] * scale_row(t, 0)
            up_pre = total[:, LANE:] * scale_row(t, 1)
            gate_sig = jax.nn.sigmoid(gate_pre)
            gate_act = gate_pre * gate_sig
            cols = pl.ds(pl.multiple_of(t * LANE, LANE), LANE)
            hid[:, cols] = (gate_act * up_pre).astype(jnp.bfloat16)
            upstream = dh[:, cols].astype(jnp.float32)
            grad_gate = upstream * up_pre * gate_sig * (1.0 + gate_pre * (1.0 - gate_sig))
            grad_up = upstream * gate_act
            ga[t, 0:slots, :] = jnp.concatenate([grad_gate, grad_up], axis=1).astype(jnp.bfloat16)
            share_across(t).start()
            share_partner(t).start()

        @pl.when(jnp.logical_and(i >= finals + 2, i < finals + 2 + tiles))
        def _():
            t = i - finals - 2
            share_across(t).wait_recv()
            forward(t).start()

        @pl.when(i >= finals + 3)
        def _():
            t = i - finals - 3
            share_partner(t).wait_recv()
            forward(t).wait_recv()
            cols = pl.ds(pl.multiple_of(t * 2 * LANE, 2 * LANE), 2 * LANE)
            for k in range(rows // depth):
                grad = jnp.dot(turned[k * depth : (k + 1) * depth, :], ga[t], preferred_element_type=jnp.float32)
                grad_ref[k * depth : (k + 1) * depth, cols] = grad.astype(jnp.bfloat16)
                for b in range(3):
                    for p in range(2):
                        n = 2 * (3 * k + b) + p
                        tile = jnp.abs(grad[b * BLK : (b + 1) * BLK, p * LANE : (p + 1) * LANE])
                        tops[n] = jnp.maximum(tops[n], jnp.max(tile.reshape(-1, SUB, LANE), axis=0))

        return carry

    lax.fori_loop(0, finals + 3 + tiles, step, 0)

    for n in range(tops.shape[0]):
        bmx[0, n : n + 1, :] = jnp.max(tops[n], axis=0, keepdims=True)
    b_copies = []
    for k in range(1, group):
        b_copies.append(
            moved(bmx.at[0], bmx.at[k], b_send.at[k - 1], b_recv.at[k - 1], {"col": lax.rem(col + k, group)})
        )
        b_copies[-1].start()

    def finish(t, carry):
        for n in (t, tiles + t):
            swap_late(n).wait_send()
            cross(n).wait_send()
        swap_early(t).wait_send()
        share_across(t).wait_send()
        share_partner(t).wait_send()
        forward(t).wait_send()
        return carry

    lax.fori_loop(0, tiles, finish, 0)
    for h in range(2):
        for n in range(4):
            y_copy(h, n).wait_send()
        for jj in range(2):
            for copy in side_copies(h, jj):
                copy.wait_send()
    for copy in b_copies:
        copy.wait()
    best = bmx[0]
    for k in range(1, group):
        best = jnp.maximum(best, bmx[k])
    block_max = jnp.max(best, axis=1, keepdims=True)
    inv_ref[...] = jnp.broadcast_to(1.0 / (block_max + epsilon), inv_ref.shape)


def update_kernel(inv_ref, cm_ref, grad_ref, hid, wv, out_hbm, update_hbm, new_hbm, uv, nv, u_sem, n_sem, h_sem):
    blocks = u_sem.shape[1]
    columns = wv.shape[2]
    tiles = columns // LANE

    def part(b):
        return pl.ds(pl.multiple_of(b * BLK, BLK), BLK)

    def put_update(b, p):
        return pltpu.make_async_copy(uv.at[p, part(b)], update_hbm.at[part(b), p, :], u_sem.at[p, b])

    def put_new(b, p):
        return pltpu.make_async_copy(nv.at[p, part(b)], new_hbm.at[part(b), p, :], n_sem.at[p, b])

    def step(b, carry):
        for p in range(2):
            inverse = inv_ref[pl.ds(2 * b + p, 1), :]
            for t in range(tiles):
                cols = slice(t * LANE, (t + 1) * LANE)
                at = (2 * t + p) * LANE
                update = grad_ref[part(b), at : at + LANE].astype(jnp.float32) * inverse
                uv[p, part(b), cols] = update
                nv[p, part(b), cols] = wv[p, part(b), cols] - (learn_rate * cm_ref[p : p + 1, cols]) * update
            put_update(b, p).start()
            put_new(b, p).start()
        return carry

    def finish(b, carry):
        for p in range(2):
            put_update(b, p).wait()
            put_new(b, p).wait()
        return carry

    put_hidden = pltpu.make_async_copy(hid, out_hbm, h_sem.at[0])
    put_hidden.start()
    lax.fori_loop(0, blocks, step, 0)
    lax.fori_loop(0, blocks, finish, 0)
    put_hidden.wait()


def on_device(tokens, routes, w_master, d_hidden):
    rows, _, columns = w_master.shape
    slots = d_hidden.shape[0]
    toks = tokens.shape[0]
    aligned = columns % LANE == 0 and rows % (12 * BLK) == 0 and slots % 32 == 0 and toks % LANE == 0
    if lax.axis_size("row") != 4 or lax.axis_size("col") != 8 or not aligned:
        return on_device_plain(tokens, routes, w_master, d_hidden)
    group = lax.axis_size("col")
    tiles = columns // LANE
    bf16, f32 = jnp.bfloat16, jnp.float32
    chunks = 6
    blocks = rows // BLK
    vmem = pl.BlockSpec(memory_space=pltpu.VMEM)
    hbm = pl.BlockSpec(memory_space=pltpu.HBM)
    dma = pltpu.SemaphoreType.DMA
    wide = 2 * LANE
    hidden, grad, colmax, inverse, master = pl.pallas_call(
        layer_kernel,
        name="layer_exchange",
        out_shape=(
            pltpu.VMEM((slots, columns), bf16),
            pltpu.VMEM((rows, 2 * columns), bf16),
            pltpu.VMEM((2, columns), f32),
            pltpu.VMEM((2 * blocks, LANE), f32),
            pltpu.VMEM((2, rows, columns), f32),
        ),
        in_specs=[hbm, hbm, hbm, hbm],
        out_specs=(vmem,) * 5,
        scratch_shapes=[
            pltpu.VMEM((2, toks), jnp.int32),
            pltpu.VMEM((slots, columns), bf16),
            pltpu.VMEM((2, toks, rows), bf16),
            pltpu.VMEM((4, toks, rows // 4), bf16),
            pltpu.VMEM((slots, rows), bf16),
            pltpu.VMEM((4, slots, rows // 4), bf16),
            pltpu.VMEM((4 * slots, rows), bf16),
            pltpu.VMEM((rows, 4 * slots), bf16),
            pltpu.VMEM((2, SUB, columns), f32),
            pltpu.VMEM((4, 2, columns), f32),
            pltpu.VMEM((tiles, rows, wide), bf16),
            pltpu.VMEM((tiles, slots, wide), bf16),
            pltpu.VMEM((tiles, slots, wide), bf16),
            pltpu.VMEM((tiles, slots, wide), f32),
            pltpu.VMEM((2 * tiles, slots // 2, wide), bf16),
            pltpu.VMEM((2 * tiles, slots // 2, wide), bf16),
            pltpu.VMEM((2, slots // 2, wide), f32),
            pltpu.VMEM((2 * tiles, slots // 2, wide), bf16),
            pltpu.VMEM((2 * tiles, slots // 2, wide), bf16),
            pltpu.VMEM((tiles, 4 * slots, wide), bf16),
            pltpu.VMEM((2 * blocks, SUB, LANE), f32),
            pltpu.VMEM((group, 2 * blocks, LANE), f32),
            dma((2,)),
            dma((6,)),
            dma((2, chunks)),
            dma((1,)),
            dma((1,)),
            dma((8,)),
            dma((8,)),
        ]
        + [dma((4,))] * 4
        + [dma((3,))] * 2
        + [dma((group - 1,))] * 2
        + [dma((2 * tiles,))] * 4
        + [dma((tiles,))] * 8,
        compiler_params=pltpu.CompilerParams(
            collective_id=0, has_side_effects=True, vmem_limit_bytes=34 * 1024 * 1024
        ),
    )(*(pltpu.with_memory_space_constraint(x, pltpu.HBM) for x in (routes.T, d_hidden, tokens, w_master)))
    hidden, update, new_master = pl.pallas_call(
        update_kernel,
        name="master_update",
        out_shape=(jax.ShapeDtypeStruct((slots, columns), bf16),)
        + (jax.ShapeDtypeStruct(w_master.shape, f32),) * 2,
        in_specs=[vmem] * 5,
        out_specs=(hbm, hbm, hbm),
        scratch_shapes=[
            pltpu.VMEM((2, rows, columns), f32),
            pltpu.VMEM((2, rows, columns), f32),
            dma((2, blocks)),
            dma((2, blocks)),
            dma((1,)),
        ],
        compiler_params=pltpu.CompilerParams(vmem_limit_bytes=30 * 1024 * 1024),
    )(inverse, colmax, grad, hidden, master)
    return (hidden, update, new_master)


def solution(mesh):
    in_specs = (P("row", None), P("row", None), P("row", None, "col"), P("row", "col"))
    out_specs = (P("row", "col"), P("row", None, "col"), P("row", None, "col"))
    return jax.shard_map(
        on_device, mesh=mesh, in_specs=in_specs, out_specs=out_specs, check_vma=False
    )
```

```python
import jax
import jax.numpy as jnp
from jax import lax
from jax.experimental import pallas as pl
from jax.experimental.pallas import tpu as pltpu
from jax.sharding import PartitionSpec as P

BLK = 128


epsilon = 1e-06
quant_range = 448.0
learn_rate = 0.05


def on_device_plain(tokens, routes, w_master, d_hidden):
    rows_local, _, columns = w_master.shape
    slots = d_hidden.shape[0]
    colmax = lax.pmax(jnp.max(jnp.abs(w_master), axis=0), "row")
    wscale = (colmax + epsilon) / quant_range
    quantized = (w_master / wscale).astype(jnp.bfloat16).reshape(rows_local, 2 * columns)
    flat_scale = wscale.reshape(2 * columns)
    routed = jnp.any(routes == 0, axis=1)
    picked = jnp.nonzero(routed, size=slots)[0].astype(jnp.int32)
    slot_rows = tokens[picked]
    slot_cols = lax.all_to_all(slot_rows, "row", split_axis=1, concat_axis=0, tiled=True)
    slot_part = lax.slice_in_dim(slot_cols, 0, lax.axis_size("row") * slots, axis=0)
    summed = lax.psum_scatter(
        jnp.dot(slot_part, quantized, preferred_element_type=jnp.float32).astype(jnp.bfloat16),
        "row",
        scatter_dimension=0,
        tiled=True,
    ).astype(jnp.float32)
    projected = (summed * flat_scale).reshape(slots, 2, columns)
    gate_pre = projected[:, 0]
    up_pre = projected[:, 1]
    gate_sig = jax.nn.sigmoid(gate_pre)
    gate_act = gate_pre * gate_sig
    hidden = (gate_act * up_pre).astype(jnp.bfloat16)
    upstream = d_hidden.astype(jnp.float32)
    grad_gate = upstream * up_pre * gate_sig * (1.0 + gate_pre * (1.0 - gate_sig))
    grad_up = upstream * gate_act
    grad_pre = (
        jnp.stack([grad_gate, grad_up], axis=1).astype(jnp.bfloat16).reshape(slots, 2 * columns)
    )
    shard_piece = lax.all_gather(grad_pre, "row", axis=0, tiled=True)
    groups = shard_piece.shape[0] // slots
    slot_part = lax.slice_in_dim(slot_cols, 0, shard_piece.shape[0], axis=0).reshape(
        groups, slots, rows_local
    )
    block_terms = jnp.einsum(
        "gsd,gsf->gdf",
        slot_part,
        shard_piece.reshape(groups, slots, 2 * columns),
        preferred_element_type=jnp.float32,
    )
    rounded = lax.optimization_barrier(block_terms.astype(jnp.bfloat16)).astype(jnp.float32)
    grad_full = jnp.sum(rounded, axis=0)
    grad_blocks = grad_full.reshape(rows_local // BLK, BLK, 2, columns)
    block_max = lax.pmax(jnp.max(jnp.abs(grad_blocks), axis=(1, 3)), "col")
    update = (grad_blocks / (block_max[:, None, :, None] + epsilon)).reshape(rows_local, 2, columns)
    new_master = w_master - learn_rate * colmax * update
    return (hidden, update, new_master)


LANE = 128
SUB = 8
LEAD = 9
SWAP = 3
SHARE = 3


def moved(src, dst, send, recv, to):
    return pltpu.make_async_remote_copy(
        src_ref=src,
        dst_ref=dst,
        send_sem=send,
        recv_sem=recv,
        device_id=to,
        device_id_type=pl.DeviceIdType.MESH,
    )


def flipped(index, bit):
    return index + bit - 2 * bit * lax.rem(index // bit, 2)


def layer_kernel(
    routes_hbm, dh_hbm, tok_hbm, w_hbm, hid, grad_ref, cm_ref, inv_ref, wv,
    routes, dh, tokv, tokq, psendt, qsend, sc, turned, folded, cmx, wq,
    esend, erec, own, lsend, lrec, keep, xsend, xrec, ga, tops, bmx,
    in_sem, tok_sem, w_sem, pt_send, pt_recv, y_send, y_recv, x_send, x_recv, z_send, z_recv,
    c_send, c_recv, b_send, b_recv, l_send, l_recv, xs_send, xs_recv,
    e_send, e_recv, ga_send, ga_recv, gp_send, gp_recv, gf_send, gf_recv,
):
    me = lax.axis_index("row")
    col = lax.axis_index("col")
    core = lax.rem(me, 2)
    partner = me + 1 - 2 * core
    across = lax.rem(me + 2, 4)
    diag = lax.rem(partner + 2, 4)
    group = bmx.shape[0]
    col_x = flipped(col, 1)
    col_z = flipped(col, 2)
    col_far = flipped(col, 4)
    quarter_of = lax.rem(col, 4)
    tiles = ga.shape[0]
    slots = hid.shape[0]
    rows = sc.shape[1]
    toks = routes.shape[1]
    chunks = w_sem.shape[1]
    piece = rows // chunks
    quarter = rows // 4
    half = slots // 2

    in_copies = (
        pltpu.make_async_copy(routes_hbm, routes, in_sem.at[0]),
        pltpu.make_async_copy(dh_hbm, dh, in_sem.at[1]),
    )
    in_copies[0].start()
    q_copies = []
    for n in range(4):
        q = (quarter_of, 3 - quarter_of)[n // 2]
        cols = pl.ds(pl.multiple_of((across, diag)[n % 2] * rows + q * quarter, LANE), quarter)
        q_copies.append(pltpu.make_async_copy(tok_hbm.at[:, cols], tokq.at[n], tok_sem.at[n]))
        q_copies[-1].start()
    w_copies = []
    for k in range(chunks):
        part = pl.ds(k * piece, piece)
        for p in range(2):
            w_copies.append(
                pltpu.make_async_copy(w_hbm.at[part, p, :], wv.at[p, part], w_sem.at[p, k])
            )
            w_copies[-1].start()
    tok_copies = []
    for n in range(2):
        cols = pl.ds(pl.multiple_of((partner, me)[n] * rows, LANE), rows)
        tok_copies.append(pltpu.make_async_copy(tok_hbm.at[:, cols], tokv.at[n], tok_sem.at[4 + n]))
        tok_copies[-1].start()
    in_copies[1].start()

    barrier = pltpu.get_barrier_semaphore()
    greeted = [{"row": r} for r in (across, diag, partner)] + [{"col": c} for c in (col_x, col_z, col_far)]
    for device in greeted:
        pl.semaphore_signal(barrier, inc=1, device_id=device, device_id_type=pl.DeviceIdType.MESH)

    before = lax.broadcasted_iota(jnp.int32, (LANE, LANE), 0)
    after = lax.broadcasted_iota(jnp.int32, (LANE, LANE), 1)
    ladder = jnp.where(before < after, 1.0, 0.0).astype(jnp.bfloat16)
    every = jnp.ones((LANE, LANE), jnp.bfloat16)
    in_copies[0].wait()
    named = jnp.logical_or(routes[0:1, :] == 0, routes[1:2, :] == 0)
    flag = jnp.where(named, 1.0, 0.0)
    mask = jnp.broadcast_to(flag, (16, toks)).astype(jnp.bfloat16)
    earlier = jnp.zeros((16, LANE), jnp.float32)
    places = []
    for k in range(toks // LANE):
        part = mask[:, k * LANE : (k + 1) * LANE]
        places.append(earlier + jnp.dot(part, ladder, preferred_element_type=jnp.float32))
        earlier = earlier + jnp.dot(part, every, preferred_element_type=jnp.float32)
    place = jnp.concatenate(places, axis=1)[0:1, :].astype(jnp.int32)
    slot_id = lax.broadcasted_iota(jnp.int32, (slots, toks), 0)
    pick = jnp.where(slot_id == place, flag, 0.0).astype(jnp.bfloat16)
    pl.semaphore_wait(barrier, len(greeted))

    def routed(h, jj, q):
        return sc.at[
            pl.ds((2 + h) * slots + jj * half, half),
            pl.ds(pl.multiple_of(q * quarter, LANE), quarter),
        ]

    def y_copy(h, n):
        return moved(
            qsend.at[n, pl.ds(h * half, half)],
            routed(h, n % 2, (quarter_of, 3 - quarter_of)[n // 2]),
            y_send.at[4 * h + n],
            y_recv.at[4 * h + n],
            {"row": (across, diag)[n % 2]},
        )

    for n in range(4):
        q_copies[n].wait()
        qsend[n] = jnp.dot(pick, tokq[n], preferred_element_type=jnp.float32).astype(jnp.bfloat16)
        y_copy(0, n).start()
    def side_copies(h, jj):
        here = routed(h, jj, quarter_of)
        n = 2 * h + jj
        return (
            moved(here, here, x_send.at[n], x_recv.at[n], {"col": col_x}),
            moved(here, here, z_send.at[n], z_recv.at[n], {"col": col_z}),
        )

    def pass_on(h, jj):
        y_copy(h, jj).wait_recv()
        for copy in side_copies(h, jj):
            copy.start()

    def arrived(h):
        for jj in range(2):
            y_copy(h, 2 + jj).wait_recv()
            for copy in side_copies(h, jj):
                copy.wait_recv()

    folded[...] = jnp.zeros(folded.shape, jnp.float32)

    def fold_chunk(k):
        for p in range(2):
            w_copies[2 * k + p].wait()

        def fold(t, carry):
            cols = pl.ds(pl.multiple_of(t * LANE, LANE), LANE)
            for p in range(2):
                tile = jnp.abs(wv[p, k * piece : (k + 1) * piece, cols])
                best = jnp.max(tile.reshape(-1, SUB, LANE), axis=0)
                folded[p, :, cols] = jnp.maximum(folded[p, :, cols], best)
            return carry

        lax.fori_loop(0, tiles, fold, 0)

    for k in range(chunks):
        fold_chunk(k)
    for p in range(2):
        cmx[0, p : p + 1, :] = jnp.max(folded[p], axis=0, keepdims=True)
    c_copies = []
    for j, row in enumerate((across, diag, partner)):
        c_copies.append(moved(cmx.at[0], cmx.at[j + 1], c_send.at[j], c_recv.at[j], {"row": row}))
        c_copies[-1].start()
    for n in range(4):
        y_copy(1, n).start()
    pass_on(0, 0)
    tok_copies[0].wait()
    psendt[...] = jnp.dot(pick, tokv[0], preferred_element_type=jnp.float32).astype(jnp.bfloat16)
    t_copy = moved(psendt, sc.at[pl.ds(slots, slots)], pt_send.at[0], pt_recv.at[0], {"row": partner})
    t_copy.start()
    pass_on(0, 1)
    tok_copies[1].wait()
    sc[0:slots, :] = jnp.dot(pick, tokv[1], preferred_element_type=jnp.float32).astype(jnp.bfloat16)
    turned[:, 0:slots] = sc[0:slots, :].T
    t_copy.wait()
    turned[:, slots : 2 * slots] = sc[slots : 2 * slots, :].T
    tops[...] = jnp.zeros(tops.shape, jnp.float32)
    in_copies[1].wait()
    for copy in c_copies:
        copy.wait()
    cm_ref[...] = jnp.maximum(jnp.maximum(cmx[0], cmx[1]), jnp.maximum(cmx[2], cmx[3]))
    arrived(0)

    def scale_row(t, p):
        cols = pl.ds(pl.multiple_of(t * LANE, LANE), LANE)
        return (cm_ref[p : p + 1, cols] + epsilon) / quant_range

    def swap_late(n):
        return moved(lsend.at[n], lrec.at[n], l_send.at[n], l_recv.at[n], {"row": partner})

    def swap_early(t):
        return moved(esend.at[t], erec.at[t], e_send.at[t], e_recv.at[t], {"row": partner})

    def cross(n):
        return moved(xsend.at[n], xrec.at[n], xs_send.at[n], xs_recv.at[n], {"row": across})

    def grad_block(t, j):
        return ga.at[t, pl.ds(j * slots, slots)]

    def share_across(t):
        return moved(grad_block(t, 0), grad_block(t, 2), ga_send.at[t], ga_recv.at[t], {"row": across})

    def share_partner(t):
        return moved(grad_block(t, 0), grad_block(t, 1), gp_send.at[t], gp_recv.at[t], {"row": partner})

    def forward(t):
        return moved(grad_block(t, 2), grad_block(t, 3), gf_send.at[t], gf_recv.at[t], {"row": partner})

    depth = 3 * BLK
    finals = tiles + LEAD

    def step(i, carry):
        @pl.when(i == 1)
        def _():
            pass_on(1, 0)

        @pl.when(i == 2)
        def _():
            pass_on(1, 1)

        @pl.when(i == tiles)
        def _():
            arrived(1)

        @pl.when(i < tiles)
        def _():
            for p in range(2):
                w = wv[p, :, pl.ds(pl.multiple_of(i * LANE, LANE), LANE)]
                wq[i, :, p * LANE : (p + 1) * LANE] = (w * (1.0 / scale_row(i, p))).astype(jnp.bfloat16)

        @pl.when(i < 2 * tiles)
        def _():
            h = i // tiles
            t = lax.rem(i, tiles)
            late = sc[pl.ds(pl.multiple_of((2 + h) * slots, 16), slots), :]
            term = jnp.dot(late, wq[t], preferred_element_type=jnp.float32)
            lsend[i] = term[half:].astype(jnp.bfloat16)
            keep[lax.rem(i, SWAP + 1)] = term[:half]
            swap_late(i).start()

        @pl.when(jnp.logical_and(i >= SWAP, i < 2 * tiles + SWAP))
        def _():
            n = i - SWAP
            swap_late(n).wait_recv()
            xsend[n] = (keep[lax.rem(n, SWAP + 1)] + lrec[n].astype(jnp.float32)).astype(jnp.bfloat16)
            cross(n).start()

        @pl.when(jnp.logical_and(i >= tiles, i < 2 * tiles))
        def _():
            t = i - tiles
            term = jnp.dot(sc[0 : 2 * slots, :], wq[t], preferred_element_type=jnp.float32)
            esend[t] = term[slots:].astype(jnp.bfloat16)
            own[t] = term[:slots]
            swap_early(t).start()

        @pl.when(i == tiles + 1)
        def _():
            for jj in range(2):
                block = [sc[(2 + h) * slots + jj * half : (2 + h) * slots + (jj + 1) * half, :] for h in range(2)]
                turned[:, (2 + jj) * slots : (3 + jj) * slots] = jnp.concatenate(block, axis=0).T

        @pl.when(jnp.logical_and(i >= finals, i < finals + tiles))
        def _():
            t = i - finals
            swap_early(t).wait_recv()
            cross(t).wait_recv()
            cross(tiles + t).wait_recv()
            others = jnp.concatenate([xrec[t], xrec[tiles + t]], axis=0).astype(jnp.float32)
            total = own[t] + erec[t].astype(jnp.float32) + others
            gate_pre = total[:, :LANE] * scale_row(t, 0)
            up_pre = total[:, LANE:] * scale_row(t, 1)
            gate_sig = jax.nn.sigmoid(gate_pre)
            gate_act = gate_pre * gate_sig
            cols = pl.ds(pl.multiple_of(t * LANE, LANE), LANE)
            hid[:, cols] = (gate_act * up_pre).astype(jnp.bfloat16)
            upstream = dh[:, cols].astype(jnp.float32)
            grad_gate = upstream * up_pre * gate_sig * (1.0 + gate_pre * (1.0 - gate_sig))
            grad_up = upstream * gate_act
            ga[t, 0:slots, :] = jnp.concatenate([grad_gate, grad_up], axis=1).astype(jnp.bfloat16)
            share_across(t).start()
            share_partner(t).start()

        @pl.when(jnp.logical_and(i >= finals + SHARE, i < finals + SHARE + tiles))
        def _():
            t = i - finals - SHARE
            share_across(t).wait_recv()
            forward(t).start()

        @pl.when(i >= finals + SHARE + 1)
        def _():
            t = i - finals - SHARE - 1
            share_partner(t).wait_recv()
            forward(t).wait_recv()
            cols = pl.ds(pl.multiple_of(t * 2 * LANE, 2 * LANE), 2 * LANE)
            for k in range(rows // depth):
                grad = jnp.dot(turned[k * depth : (k + 1) * depth, :], ga[t], preferred_element_type=jnp.float32)
                grad_ref[k * depth : (k + 1) * depth, cols] = grad.astype(jnp.bfloat16)
                for b in range(3):
                    for p in range(2):
                        n = 2 * (3 * k + b) + p
                        tile = jnp.abs(grad[b * BLK : (b + 1) * BLK, p * LANE : (p + 1) * LANE])
                        tops[n] = jnp.maximum(tops[n], jnp.max(tile.reshape(-1, SUB, LANE), axis=0))

        return carry

    lax.fori_loop(0, finals + SHARE + 1 + tiles, step, 0)

    for n in range(tops.shape[0]):
        bmx[0, n : n + 1, :] = jnp.max(tops[n], axis=0, keepdims=True)
    b_copies = []
    for k in range(1, group):
        b_copies.append(
            moved(bmx.at[0], bmx.at[k], b_send.at[k - 1], b_recv.at[k - 1], {"col": lax.rem(col + k, group)})
        )
        b_copies[-1].start()

    def finish(t, carry):
        for n in (t, tiles + t):
            swap_late(n).wait_send()
            cross(n).wait_send()
        swap_early(t).wait_send()
        share_across(t).wait_send()
        share_partner(t).wait_send()
        forward(t).wait_send()
        return carry

    lax.fori_loop(0, tiles, finish, 0)
    for h in range(2):
        for n in range(4):
            y_copy(h, n).wait_send()
        for jj in range(2):
            for copy in side_copies(h, jj):
                copy.wait_send()
    for copy in b_copies:
        copy.wait()
    best = bmx[0]
    for k in range(1, group):
        best = jnp.maximum(best, bmx[k])
    block_max = jnp.max(best, axis=1, keepdims=True)
    inv_ref[...] = jnp.broadcast_to(1.0 / (block_max + epsilon), inv_ref.shape)


def update_kernel(inv_ref, cm_ref, grad_ref, hid, wv, out_hbm, update_hbm, new_hbm, uv, nv, u_sem, n_sem, h_sem):
    blocks = u_sem.shape[1]
    columns = wv.shape[2]
    tiles = columns // LANE

    def part(b):
        return pl.ds(pl.multiple_of(b * BLK, BLK), BLK)

    def put_update(b, p):
        return pltpu.make_async_copy(uv.at[p, part(b)], update_hbm.at[part(b), p, :], u_sem.at[p, b])

    def put_new(b, p):
        return pltpu.make_async_copy(nv.at[p, part(b)], new_hbm.at[part(b), p, :], n_sem.at[p, b])

    def step(b, carry):
        for p in range(2):
            inverse = inv_ref[pl.ds(2 * b + p, 1), :]
            for t in range(tiles):
                cols = slice(t * LANE, (t + 1) * LANE)
                at = (2 * t + p) * LANE
                update = grad_ref[part(b), at : at + LANE].astype(jnp.float32) * inverse
                uv[p, part(b), cols] = update
                nv[p, part(b), cols] = wv[p, part(b), cols] - (learn_rate * cm_ref[p : p + 1, cols]) * update
            put_update(b, p).start()
            put_new(b, p).start()
        return carry

    def finish(b, carry):
        for p in range(2):
            put_update(b, p).wait()
            put_new(b, p).wait()
        return carry

    put_hidden = pltpu.make_async_copy(hid, out_hbm, h_sem.at[0])
    put_hidden.start()
    lax.fori_loop(0, blocks, step, 0)
    lax.fori_loop(0, blocks, finish, 0)
    put_hidden.wait()


def on_device(tokens, routes, w_master, d_hidden):
    rows, _, columns = w_master.shape
    slots = d_hidden.shape[0]
    toks = tokens.shape[0]
    aligned = columns % LANE == 0 and rows % (12 * BLK) == 0 and slots % 32 == 0 and toks % LANE == 0
    if lax.axis_size("row") != 4 or lax.axis_size("col") != 8 or not aligned:
        return on_device_plain(tokens, routes, w_master, d_hidden)
    group = lax.axis_size("col")
    tiles = columns // LANE
    bf16, f32 = jnp.bfloat16, jnp.float32
    chunks = 6
    blocks = rows // BLK
    vmem = pl.BlockSpec(memory_space=pltpu.VMEM)
    hbm = pl.BlockSpec(memory_space=pltpu.HBM)
    dma = pltpu.SemaphoreType.DMA
    wide = 2 * LANE
    hidden, grad, colmax, inverse, master = pl.pallas_call(
        layer_kernel,
        name="layer_exchange",
        out_shape=(
            pltpu.VMEM((slots, columns), bf16),
            pltpu.VMEM((rows, 2 * columns), bf16),
            pltpu.VMEM((2, columns), f32),
            pltpu.VMEM((2 * blocks, LANE), f32),
            pltpu.VMEM((2, rows, columns), f32),
        ),
        in_specs=[hbm, hbm, hbm, hbm],
        out_specs=(vmem,) * 5,
        scratch_shapes=[
            pltpu.VMEM((2, toks), jnp.int32),
            pltpu.VMEM((slots, columns), bf16),
            pltpu.VMEM((2, toks, rows), bf16),
            pltpu.VMEM((4, toks, rows // 4), bf16),
            pltpu.VMEM((slots, rows), bf16),
            pltpu.VMEM((4, slots, rows // 4), bf16),
            pltpu.VMEM((4 * slots, rows), bf16),
            pltpu.VMEM((rows, 4 * slots), bf16),
            pltpu.VMEM((2, SUB, columns), f32),
            pltpu.VMEM((4, 2, columns), f32),
            pltpu.VMEM((tiles, rows, wide), bf16),
            pltpu.VMEM((tiles, slots, wide), bf16),
            pltpu.VMEM((tiles, slots, wide), bf16),
            pltpu.VMEM((tiles, slots, wide), f32),
            pltpu.VMEM((2 * tiles, slots // 2, wide), bf16),
            pltpu.VMEM((2 * tiles, slots // 2, wide), bf16),
            pltpu.VMEM((SWAP + 1, slots // 2, wide), f32),
            pltpu.VMEM((2 * tiles, slots // 2, wide), bf16),
            pltpu.VMEM((2 * tiles, slots // 2, wide), bf16),
            pltpu.VMEM((tiles, 4 * slots, wide), bf16),
            pltpu.VMEM((2 * blocks, SUB, LANE), f32),
            pltpu.VMEM((group, 2 * blocks, LANE), f32),
            dma((2,)),
            dma((6,)),
            dma((2, chunks)),
            dma((1,)),
            dma((1,)),
            dma((8,)),
            dma((8,)),
        ]
        + [dma((4,))] * 4
        + [dma((3,))] * 2
        + [dma((group - 1,))] * 2
        + [dma((2 * tiles,))] * 4
        + [dma((tiles,))] * 8,
        compiler_params=pltpu.CompilerParams(
            collective_id=0, has_side_effects=True, vmem_limit_bytes=34 * 1024 * 1024
        ),
    )(*(pltpu.with_memory_space_constraint(x, pltpu.HBM) for x in (routes.T, d_hidden, tokens, w_master)))
    hidden, update, new_master = pl.pallas_call(
        update_kernel,
        name="master_update",
        out_shape=(jax.ShapeDtypeStruct((slots, columns), bf16),)
        + (jax.ShapeDtypeStruct(w_master.shape, f32),) * 2,
        in_specs=[vmem] * 5,
        out_specs=(hbm, hbm, hbm),
        scratch_shapes=[
            pltpu.VMEM((2, rows, columns), f32),
            pltpu.VMEM((2, rows, columns), f32),
            dma((2, blocks)),
            dma((2, blocks)),
            dma((1,)),
        ],
        compiler_params=pltpu.CompilerParams(vmem_limit_bytes=30 * 1024 * 1024),
    )(inverse, colmax, grad, hidden, master)
    return (hidden, update, new_master)


def solution(mesh):
    in_specs = (P("row", None), P("row", None), P("row", None, "col"), P("row", "col"))
    out_specs = (P("row", "col"), P("row", None, "col"), P("row", None, "col"))
    return jax.shard_map(
        on_device, mesh=mesh, in_specs=in_specs, out_specs=out_specs, check_vma=False
    )
```

```python
import jax
import jax.numpy as jnp
from jax import lax
from jax.experimental import pallas as pl
from jax.experimental.pallas import tpu as pltpu
from jax.sharding import PartitionSpec as P

BLK = 128


epsilon = 1e-06
quant_range = 448.0
learn_rate = 0.05


def on_device_plain(tokens, routes, w_master, d_hidden):
    rows_local, _, columns = w_master.shape
    slots = d_hidden.shape[0]
    colmax = lax.pmax(jnp.max(jnp.abs(w_master), axis=0), "row")
    wscale = (colmax + epsilon) / quant_range
    quantized = (w_master / wscale).astype(jnp.bfloat16).reshape(rows_local, 2 * columns)
    flat_scale = wscale.reshape(2 * columns)
    routed = jnp.any(routes == 0, axis=1)
    picked = jnp.nonzero(routed, size=slots)[0].astype(jnp.int32)
    slot_rows = tokens[picked]
    slot_cols = lax.all_to_all(slot_rows, "row", split_axis=1, concat_axis=0, tiled=True)
    slot_part = lax.slice_in_dim(slot_cols, 0, lax.axis_size("row") * slots, axis=0)
    summed = lax.psum_scatter(
        jnp.dot(slot_part, quantized, preferred_element_type=jnp.float32).astype(jnp.bfloat16),
        "row",
        scatter_dimension=0,
        tiled=True,
    ).astype(jnp.float32)
    projected = (summed * flat_scale).reshape(slots, 2, columns)
    gate_pre = projected[:, 0]
    up_pre = projected[:, 1]
    gate_sig = jax.nn.sigmoid(gate_pre)
    gate_act = gate_pre * gate_sig
    hidden = (gate_act * up_pre).astype(jnp.bfloat16)
    upstream = d_hidden.astype(jnp.float32)
    grad_gate = upstream * up_pre * gate_sig * (1.0 + gate_pre * (1.0 - gate_sig))
    grad_up = upstream * gate_act
    grad_pre = (
        jnp.stack([grad_gate, grad_up], axis=1).astype(jnp.bfloat16).reshape(slots, 2 * columns)
    )
    shard_piece = lax.all_gather(grad_pre, "row", axis=0, tiled=True)
    groups = shard_piece.shape[0] // slots
    slot_part = lax.slice_in_dim(slot_cols, 0, shard_piece.shape[0], axis=0).reshape(
        groups, slots, rows_local
    )
    block_terms = jnp.einsum(
        "gsd,gsf->gdf",
        slot_part,
        shard_piece.reshape(groups, slots, 2 * columns),
        preferred_element_type=jnp.float32,
    )
    rounded = lax.optimization_barrier(block_terms.astype(jnp.bfloat16)).astype(jnp.float32)
    grad_full = jnp.sum(rounded, axis=0)
    grad_blocks = grad_full.reshape(rows_local // BLK, BLK, 2, columns)
    block_max = lax.pmax(jnp.max(jnp.abs(grad_blocks), axis=(1, 3)), "col")
    update = (grad_blocks / (block_max[:, None, :, None] + epsilon)).reshape(rows_local, 2, columns)
    new_master = w_master - learn_rate * colmax * update
    return (hidden, update, new_master)


LANE = 128
SUB = 8
CUT = (1, 2)
FIRST = 3
SWAP = 1
SHARE = 4


def moved(src, dst, send, recv, to):
    return pltpu.make_async_remote_copy(
        src_ref=src,
        dst_ref=dst,
        send_sem=send,
        recv_sem=recv,
        device_id=to,
        device_id_type=pl.DeviceIdType.MESH,
    )


def wide_part(slots):
    return slots - slots * CUT[0] // CUT[1] // 16 * 16


def flipped(index, bit):
    return index + bit - 2 * bit * lax.rem(index // bit, 2)


def layer_kernel(
    routes_hbm, dh_hbm, tok_hbm, w_hbm, hid, grad_ref, cm_ref, inv_ref, wv,
    routes, dh, tokv, tokq, psendt, qsend, sc, turned, folded, cmx, wq,
    esend, erec, own, lsend, lrec, keep, xsend, xrec, ga, tops, flat, bmx,
    in_sem, tok_sem, w_sem, pt_send, pt_recv, y_send, y_recv, x_send, x_recv, z_send, z_recv,
    c_send, c_recv, b_send, b_recv, l_send, l_recv, xs_send, xs_recv,
    ga_send, ga_recv, gp_send, gp_recv, gf_send, gf_recv, e_send, e_recv,
):
    me = lax.axis_index("row")
    col = lax.axis_index("col")
    core = lax.rem(me, 2)
    partner = me + 1 - 2 * core
    across = lax.rem(me + 2, 4)
    diag = lax.rem(partner + 2, 4)
    group = bmx.shape[0]
    col_x = flipped(col, 1)
    col_z = flipped(col, 2)
    col_far = flipped(col, 4)
    quarter_of = lax.rem(col, 4)
    tiles = ga.shape[0]
    slots = hid.shape[0]
    rows = sc.shape[1]
    toks = routes.shape[1]
    chunks = w_sem.shape[1]
    piece = rows // chunks
    quarter = rows // 4
    sizes = (slots - wide_part(slots), wide_part(slots))
    starts = (0, sizes[0])
    bases = (2 * slots, 2 * slots + 2 * sizes[0])

    in_copies = (
        pltpu.make_async_copy(routes_hbm, routes, in_sem.at[0]),
        pltpu.make_async_copy(dh_hbm, dh, in_sem.at[1]),
    )
    in_copies[0].start()
    q_copies = []
    for n in range(4):
        q = (quarter_of, 3 - quarter_of)[n // 2]
        cols = pl.ds(pl.multiple_of((across, diag)[n % 2] * rows + q * quarter, LANE), quarter)
        q_copies.append(pltpu.make_async_copy(tok_hbm.at[:, cols], tokq.at[n], tok_sem.at[n]))
        q_copies[-1].start()
    tok_copies = []
    for n in range(2):
        cols = pl.ds(pl.multiple_of((partner, me)[n] * rows, LANE), rows)
        tok_copies.append(pltpu.make_async_copy(tok_hbm.at[:, cols], tokv.at[n], tok_sem.at[4 + n]))
        tok_copies[-1].start()
    w_copies = []
    for k in range(chunks):
        part = pl.ds(k * piece, piece)
        for p in range(2):
            w_copies.append(
                pltpu.make_async_copy(w_hbm.at[part, p, :], wv.at[p, part], w_sem.at[p, k])
            )
            w_copies[-1].start()
    in_copies[1].start()

    barrier = pltpu.get_barrier_semaphore()
    greeted = [{"row": r} for r in (across, diag, partner)] + [{"col": c} for c in (col_x, col_z, col_far)]
    for device in greeted:
        pl.semaphore_signal(barrier, inc=1, device_id=device, device_id_type=pl.DeviceIdType.MESH)

    before = lax.broadcasted_iota(jnp.int32, (LANE, LANE), 0)
    after = lax.broadcasted_iota(jnp.int32, (LANE, LANE), 1)
    ladder = jnp.where(before < after, 1.0, 0.0).astype(jnp.bfloat16)
    every = jnp.ones((LANE, LANE), jnp.bfloat16)
    in_copies[0].wait()
    named = jnp.logical_or(routes[0:1, :] == 0, routes[1:2, :] == 0)
    flag = jnp.where(named, 1.0, 0.0)
    mask = jnp.broadcast_to(flag, (16, toks)).astype(jnp.bfloat16)
    earlier = jnp.zeros((16, LANE), jnp.float32)
    places = []
    for k in range(toks // LANE):
        part = mask[:, k * LANE : (k + 1) * LANE]
        places.append(earlier + jnp.dot(part, ladder, preferred_element_type=jnp.float32))
        earlier = earlier + jnp.dot(part, every, preferred_element_type=jnp.float32)
    place = jnp.concatenate(places, axis=1)[0:1, :].astype(jnp.int32)
    slot_id = lax.broadcasted_iota(jnp.int32, (slots, toks), 0)
    pick = jnp.where(slot_id == place, flag, 0.0).astype(jnp.bfloat16)
    pl.semaphore_wait(barrier, len(greeted))

    def routed(h, jj, q):
        return sc.at[
            pl.ds(bases[h] + jj * sizes[h], sizes[h]),
            pl.ds(pl.multiple_of(q * quarter, LANE), quarter),
        ]

    def y_copy(h, n):
        return moved(
            qsend.at[n, pl.ds(starts[h], sizes[h])],
            routed(h, n % 2, (quarter_of, 3 - quarter_of)[n // 2]),
            y_send.at[4 * h + n],
            y_recv.at[4 * h + n],
            {"row": (across, diag)[n % 2]},
        )

    for n in range(4):
        q_copies[n].wait()
        many = slots if n < 2 else sizes[0]
        qsend[n, 0:many] = jnp.dot(pick[0:many], tokq[n], preferred_element_type=jnp.float32).astype(jnp.bfloat16)
        y_copy(0, n).start()
    def side_copies(h, jj):
        here = routed(h, jj, quarter_of)
        n = 2 * h + jj
        return (
            moved(here, here, x_send.at[n], x_recv.at[n], {"col": col_x}),
            moved(here, here, z_send.at[n], z_recv.at[n], {"col": col_z}),
        )

    def pass_on(h, jj):
        y_copy(h, jj).wait_recv()
        for copy in side_copies(h, jj):
            copy.start()

    def relay_x():
        block = routed(1, 1, lax.rem(col_z, 4))
        return moved(block, block, x_send.at[4], x_recv.at[4], {"col": col_x})

    def relay_z():
        block = routed(1, 0, lax.rem(col_x, 4))
        return moved(block, block, z_send.at[4], z_recv.at[4], {"col": col_z})

    def arrived_first():
        for jj in range(2):
            y_copy(0, 2 + jj).wait_recv()
            for copy in side_copies(0, jj):
                copy.wait_recv()

    def arrived_second():
        side_copies(1, 1)[0].wait_recv()
        side_copies(1, 0)[1].wait_recv()
        relay_z().wait_recv()
        relay_x().wait_recv()

    folded[...] = jnp.zeros(folded.shape, jnp.float32)

    def fold_chunk(k):
        for p in range(2):
            w_copies[2 * k + p].wait()

        def fold(t, carry):
            cols = pl.ds(pl.multiple_of(t * LANE, LANE), LANE)
            for p in range(2):
                tile = jnp.abs(wv[p, k * piece : (k + 1) * piece, cols])
                best = jnp.max(tile.reshape(-1, SUB, LANE), axis=0)
                folded[p, :, cols] = jnp.maximum(folded[p, :, cols], best)
            return carry

        lax.fori_loop(0, tiles, fold, 0)

    tok_copies[0].wait()
    psendt[...] = jnp.dot(pick, tokv[0], preferred_element_type=jnp.float32).astype(jnp.bfloat16)
    t_copy = moved(psendt, sc.at[pl.ds(slots, slots)], pt_send.at[0], pt_recv.at[0], {"row": partner})
    t_copy.start()
    tok_copies[1].wait()
    sc[0:slots, :] = jnp.dot(pick, tokv[1], preferred_element_type=jnp.float32).astype(jnp.bfloat16)
    pass_on(0, 0)
    fold_chunk(0)
    fold_chunk(1)
    turned[:, 0:slots] = sc[0:slots, :].T
    pass_on(0, 1)
    for k in range(2, chunks):
        fold_chunk(k)
    for p in range(2):
        cmx[0, p : p + 1, :] = jnp.max(folded[p], axis=0, keepdims=True)
    c_copies = []
    for j, row in enumerate((across, diag, partner)):
        c_copies.append(moved(cmx.at[0], cmx.at[j + 1], c_send.at[j], c_recv.at[j], {"row": row}))
        c_copies[-1].start()
    for n in range(2):
        y_copy(1, n).start()
    t_copy.wait()
    turned[:, slots : 2 * slots] = sc[slots : 2 * slots, :].T
    tops[...] = jnp.zeros(tops.shape, jnp.float32)
    in_copies[1].wait()
    for copy in c_copies:
        copy.wait()
    cm_ref[...] = jnp.maximum(jnp.maximum(cmx[0], cmx[1]), jnp.maximum(cmx[2], cmx[3]))
    arrived_first()

    def scale_row(t, p):
        cols = pl.ds(pl.multiple_of(t * LANE, LANE), LANE)
        return (cm_ref[p : p + 1, cols] + epsilon) / quant_range

    def swap_late(h, t):
        n, some = h * tiles + t, pl.ds(0, sizes[h])
        return moved(lsend.at[n, some], lrec.at[n, some], l_send.at[n], l_recv.at[n], {"row": partner})

    def swap_early(t):
        return moved(esend.at[t], erec.at[t], e_send.at[t], e_recv.at[t], {"row": partner})

    def cross(h, t):
        n, some = h * tiles + t, pl.ds(0, sizes[h])
        return moved(xsend.at[n, some], xrec.at[n, some], xs_send.at[n], xs_recv.at[n], {"row": across})

    def grad_block(h, t, j):
        return ga.at[t, pl.ds(j * slots + starts[h], sizes[h])]

    def share_across(h, t):
        n = h * tiles + t
        return moved(grad_block(h, t, 0), grad_block(h, t, 2), ga_send.at[n], ga_recv.at[n], {"row": across})

    def share_partner(h, t):
        n = h * tiles + t
        return moved(grad_block(h, t, 0), grad_block(h, t, 1), gp_send.at[n], gp_recv.at[n], {"row": partner})

    def forward(h, t):
        n = h * tiles + t
        return moved(grad_block(h, t, 2), grad_block(h, t, 3), gf_send.at[n], gf_recv.at[n], {"row": partner})

    def offer(h, t, term):
        n, size = h * tiles + t, sizes[h]
        lsend[n, 0:size] = term[size:].astype(jnp.bfloat16)
        swap_late(h, t).start()
        keep[lax.rem(n, SWAP + 1), 0:size] = term[:size]

    def cross_late(h, t):
        n, size = h * tiles + t, sizes[h]
        swap_late(h, t).wait_recv()
        both = keep[lax.rem(n, SWAP + 1), 0:size] + lrec[n, 0:size].astype(jnp.float32)
        xsend[n, 0:size] = both.astype(jnp.bfloat16)
        cross(h, t).start()

    def finalize(h, t):
        mine = slice(starts[h], starts[h] + sizes[h])
        cross(h, t).wait_recv()
        others = xrec[h * tiles + t, 0 : sizes[h]].astype(jnp.float32)
        total = own[t, mine] + erec[t, mine].astype(jnp.float32) + others
        gate_pre = total[:, :LANE] * scale_row(t, 0)
        up_pre = total[:, LANE:] * scale_row(t, 1)
        gate_sig = jax.nn.sigmoid(gate_pre)
        gate_act = gate_pre * gate_sig
        cols = pl.ds(pl.multiple_of(t * LANE, LANE), LANE)
        hid[mine, cols] = (gate_act * up_pre).astype(jnp.bfloat16)
        upstream = dh[mine, cols].astype(jnp.float32)
        grad_gate = upstream * up_pre * gate_sig * (1.0 + gate_pre * (1.0 - gate_sig))
        grad_up = upstream * gate_act
        ga[t, mine, :] = jnp.concatenate([grad_gate, grad_up], axis=1).astype(jnp.bfloat16)
        share_across(h, t).start()
        share_partner(h, t).start()

    def hand_over(h, t):
        share_across(h, t).wait_recv()
        forward(h, t).start()

    depth = 3 * BLK
    first_final = SWAP + FIRST
    second = tiles + 1
    second_final = second + tiles + SWAP
    second_share = second_final + SHARE
    last = second_share + 1 + tiles

    def during(i, start):
        return jnp.logical_and(i >= start, i < start + tiles)

    def step(i, carry):
        @pl.when(i == 2)
        def _():
            pass_on(1, 0)

        @pl.when(i == 3)
        def _():
            pass_on(1, 1)

        @pl.when(i == 5)
        def _():
            side_copies(1, 0)[0].wait_recv()
            relay_z().start()

        @pl.when(i == 7)
        def _():
            side_copies(1, 1)[1].wait_recv()
            relay_x().start()

        @pl.when(i < tiles)
        def _():
            for p in range(2):
                w = wv[p, :, pl.ds(pl.multiple_of(i * LANE, LANE), LANE)]
                wq[i, :, p * LANE : (p + 1) * LANE] = (w * (1.0 / scale_row(i, p))).astype(jnp.bfloat16)
            term = jnp.dot(sc[0 : bases[1], :], wq[i], preferred_element_type=jnp.float32)
            offer(0, i, term[2 * slots :])
            esend[i] = term[slots : 2 * slots].astype(jnp.bfloat16)
            swap_early(i).start()
            own[i] = term[:slots]

        @pl.when(during(i, SWAP))
        def _():
            cross_late(0, i - SWAP)

        @pl.when(during(i, first_final))
        def _():
            t = i - first_final
            swap_early(t).wait_recv()
            finalize(0, t)

        @pl.when(i == second)
        def _():
            arrived_second()

        @pl.when(during(i, second))
        def _():
            t = i - second
            offer(1, t, jnp.dot(sc[bases[1] :, :], wq[t], preferred_element_type=jnp.float32))

        @pl.when(during(i, second + SWAP))
        def _():
            cross_late(1, i - second - SWAP)

        @pl.when(i == second + 1)
        def _():
            for jj in range(2):
                block = [sc[bases[h] + jj * sizes[h] : bases[h] + (jj + 1) * sizes[h], :] for h in range(2)]
                turned[:, (2 + jj) * slots : (3 + jj) * slots] = jnp.concatenate(block, axis=0).T

        @pl.when(during(i, second + SWAP))
        def _():
            hand_over(0, i - second - SWAP)

        @pl.when(during(i, second_final))
        def _():
            finalize(1, i - second_final)

        @pl.when(during(i, second_share))
        def _():
            hand_over(1, i - second_share)

        @pl.when(i >= second_share + 1)
        def _():
            t = i - second_share - 1
            for h in range(2):
                share_partner(h, t).wait_recv()
                forward(h, t).wait_recv()
            cols = pl.ds(pl.multiple_of(t * 2 * LANE, 2 * LANE), 2 * LANE)
            for k in range(rows // depth):
                grad = jnp.dot(turned[k * depth : (k + 1) * depth, :], ga[t], preferred_element_type=jnp.float32)
                grad_ref[k * depth : (k + 1) * depth, cols] = grad.astype(jnp.bfloat16)
                for b in range(3):
                    for p in range(2):
                        n = 2 * (3 * k + b) + p
                        tile = jnp.abs(grad[b * BLK : (b + 1) * BLK, p * LANE : (p + 1) * LANE])
                        tops[n] = jnp.maximum(tops[n], jnp.max(tile.reshape(-1, SUB, LANE), axis=0))

        return carry

    lax.fori_loop(0, last, step, 0)

    for n in range(tops.shape[0]):
        flat[n : n + 1, :] = jnp.max(tops[n], axis=0, keepdims=True)
    lane = lax.broadcasted_iota(jnp.int32, (SUB, LANE), 1)
    packs = tops.shape[0] // SUB
    packed = jnp.zeros((SUB, LANE), jnp.float32)
    for k in range(packs):
        widest = jnp.max(flat[k * SUB : (k + 1) * SUB, :], axis=1, keepdims=True)
        packed = jnp.where(lane == k, widest, packed)
    bmx[0] = packed
    b_copies = []
    for k in range(1, group):
        b_copies.append(
            moved(bmx.at[0], bmx.at[k], b_send.at[k - 1], b_recv.at[k - 1], {"col": lax.rem(col + k, group)})
        )
        b_copies[-1].start()

    def finish(t, carry):
        swap_early(t).wait_send()
        for h in range(2):
            for copy in (swap_late, cross, share_across, share_partner, forward):
                copy(h, t).wait_send()
        return carry

    lax.fori_loop(0, tiles, finish, 0)
    relay_x().wait_send()
    relay_z().wait_send()
    for h in range(2):
        for n in range(4 - 2 * h):
            y_copy(h, n).wait_send()
        for jj in range(2):
            for copy in side_copies(h, jj):
                copy.wait_send()
    for copy in b_copies:
        copy.wait()
    best = bmx[0]
    for k in range(1, group):
        best = jnp.maximum(best, bmx[k])
    for k in range(packs):
        block_max = jnp.max(jnp.where(lane == k, best, 0.0), axis=1, keepdims=True)
        inv_ref[k * SUB : (k + 1) * SUB, :] = jnp.broadcast_to(1.0 / (block_max + epsilon), (SUB, LANE))


def update_kernel(inv_ref, cm_ref, grad_ref, hid, wv, out_hbm, update_hbm, new_hbm, uv, nv, u_sem, n_sem, h_sem):
    blocks = u_sem.shape[1]
    columns = wv.shape[2]
    tiles = columns // LANE

    def part(b):
        return pl.ds(pl.multiple_of(b * BLK, BLK), BLK)

    def put_update(b, p):
        return pltpu.make_async_copy(uv.at[p, part(b)], update_hbm.at[part(b), p, :], u_sem.at[p, b])

    def put_new(b, p):
        return pltpu.make_async_copy(nv.at[p, part(b)], new_hbm.at[part(b), p, :], n_sem.at[p, b])

    def step(b, carry):
        for p in range(2):
            inverse = inv_ref[pl.ds(2 * b + p, 1), :]
            for t in range(tiles):
                cols = slice(t * LANE, (t + 1) * LANE)
                at = (2 * t + p) * LANE
                update = grad_ref[part(b), at : at + LANE].astype(jnp.float32) * inverse
                uv[p, part(b), cols] = update
                nv[p, part(b), cols] = wv[p, part(b), cols] - (learn_rate * cm_ref[p : p + 1, cols]) * update
            put_update(b, p).start()
            put_new(b, p).start()
        return carry

    def finish(b, carry):
        for p in range(2):
            put_update(b, p).wait()
            put_new(b, p).wait()
        return carry

    put_hidden = pltpu.make_async_copy(hid, out_hbm, h_sem.at[0])
    put_hidden.start()
    lax.fori_loop(0, blocks, step, 0)
    lax.fori_loop(0, blocks, finish, 0)
    put_hidden.wait()


def on_device(tokens, routes, w_master, d_hidden):
    rows, _, columns = w_master.shape
    slots = d_hidden.shape[0]
    toks = tokens.shape[0]
    aligned = columns % LANE == 0 and rows % (12 * BLK) == 0 and slots % 32 == 0 and toks % LANE == 0
    aligned = aligned and 2 * rows // BLK <= SUB * LANE
    if lax.axis_size("row") != 4 or lax.axis_size("col") != 8 or not aligned:
        return on_device_plain(tokens, routes, w_master, d_hidden)
    group = lax.axis_size("col")
    tiles = columns // LANE
    bf16, f32 = jnp.bfloat16, jnp.float32
    chunks = 6
    blocks = rows // BLK
    vmem = pl.BlockSpec(memory_space=pltpu.VMEM)
    hbm = pl.BlockSpec(memory_space=pltpu.HBM)
    dma = pltpu.SemaphoreType.DMA
    wide = 2 * LANE
    hidden, grad, colmax, inverse, master = pl.pallas_call(
        layer_kernel,
        name="layer_exchange",
        out_shape=(
            pltpu.VMEM((slots, columns), bf16),
            pltpu.VMEM((rows, 2 * columns), bf16),
            pltpu.VMEM((2, columns), f32),
            pltpu.VMEM((2 * blocks, LANE), f32),
            pltpu.VMEM((2, rows, columns), f32),
        ),
        in_specs=[hbm, hbm, hbm, hbm],
        out_specs=(vmem,) * 5,
        scratch_shapes=[
            pltpu.VMEM((2, toks), jnp.int32),
            pltpu.VMEM((slots, columns), bf16),
            pltpu.VMEM((2, toks, rows), bf16),
            pltpu.VMEM((4, toks, rows // 4), bf16),
            pltpu.VMEM((slots, rows), bf16),
            pltpu.VMEM((4, slots, rows // 4), bf16),
            pltpu.VMEM((4 * slots, rows), bf16),
            pltpu.VMEM((rows, 4 * slots), bf16),
            pltpu.VMEM((2, SUB, columns), f32),
            pltpu.VMEM((4, 2, columns), f32),
            pltpu.VMEM((tiles, rows, wide), bf16),
            pltpu.VMEM((tiles, slots, wide), bf16),
            pltpu.VMEM((tiles, slots, wide), bf16),
            pltpu.VMEM((tiles, slots, wide), f32),
            pltpu.VMEM((2 * tiles, wide_part(slots), wide), bf16),
            pltpu.VMEM((2 * tiles, wide_part(slots), wide), bf16),
            pltpu.VMEM((SWAP + 1, wide_part(slots), wide), f32),
            pltpu.VMEM((2 * tiles, wide_part(slots), wide), bf16),
            pltpu.VMEM((2 * tiles, wide_part(slots), wide), bf16),
            pltpu.VMEM((tiles, 4 * slots, wide), bf16),
            pltpu.VMEM((2 * blocks, SUB, LANE), f32),
            pltpu.VMEM((2 * blocks, LANE), f32),
            pltpu.VMEM((group, SUB, LANE), f32),
            dma((2,)),
            dma((6,)),
            dma((2, chunks)),
            dma((1,)),
            dma((1,)),
            dma((6,)),
            dma((6,)),
        ]
        + [dma((5,))] * 4
        + [dma((3,))] * 2
        + [dma((group - 1,))] * 2
        + [dma((2 * tiles,))] * 10
        + [dma((tiles,))] * 2,
        compiler_params=pltpu.CompilerParams(
            collective_id=0, has_side_effects=True, vmem_limit_bytes=34 * 1024 * 1024
        ),
    )(*(pltpu.with_memory_space_constraint(x, pltpu.HBM) for x in (routes.T, d_hidden, tokens, w_master)))
    hidden, update, new_master = pl.pallas_call(
        update_kernel,
        name="master_update",
        out_shape=(jax.ShapeDtypeStruct((slots, columns), bf16),)
        + (jax.ShapeDtypeStruct(w_master.shape, f32),) * 2,
        in_specs=[vmem] * 5,
        out_specs=(hbm, hbm, hbm),
        scratch_shapes=[
            pltpu.VMEM((2, rows, columns), f32),
            pltpu.VMEM((2, rows, columns), f32),
            dma((2, blocks)),
            dma((2, blocks)),
            dma((1,)),
        ],
        compiler_params=pltpu.CompilerParams(vmem_limit_bytes=30 * 1024 * 1024),
    )(inverse, colmax, grad, hidden, master)
    return (hidden, update, new_master)


def solution(mesh):
    in_specs = (P("row", None), P("row", None), P("row", None, "col"), P("row", "col"))
    out_specs = (P("row", "col"), P("row", None, "col"), P("row", None, "col"))
    return jax.shard_map(
        on_device, mesh=mesh, in_specs=in_specs, out_specs=out_specs, check_vma=False
    )
```

```python
import jax
import jax.numpy as jnp
from jax import lax
from jax.experimental import pallas as pl
from jax.experimental.pallas import tpu as pltpu
from jax.sharding import PartitionSpec as P

BLK = 128


epsilon = 1e-06
quant_range = 448.0
learn_rate = 0.05


def on_device_plain(tokens, routes, w_master, d_hidden):
    rows_local, _, columns = w_master.shape
    slots = d_hidden.shape[0]
    colmax = lax.pmax(jnp.max(jnp.abs(w_master), axis=0), "row")
    wscale = (colmax + epsilon) / quant_range
    quantized = (w_master / wscale).astype(jnp.bfloat16).reshape(rows_local, 2 * columns)
    flat_scale = wscale.reshape(2 * columns)
    routed = jnp.any(routes == 0, axis=1)
    picked = jnp.nonzero(routed, size=slots)[0].astype(jnp.int32)
    slot_rows = tokens[picked]
    slot_cols = lax.all_to_all(slot_rows, "row", split_axis=1, concat_axis=0, tiled=True)
    slot_part = lax.slice_in_dim(slot_cols, 0, lax.axis_size("row") * slots, axis=0)
    summed = lax.psum_scatter(
        jnp.dot(slot_part, quantized, preferred_element_type=jnp.float32).astype(jnp.bfloat16),
        "row",
        scatter_dimension=0,
        tiled=True,
    ).astype(jnp.float32)
    projected = (summed * flat_scale).reshape(slots, 2, columns)
    gate_pre = projected[:, 0]
    up_pre = projected[:, 1]
    gate_sig = jax.nn.sigmoid(gate_pre)
    gate_act = gate_pre * gate_sig
    hidden = (gate_act * up_pre).astype(jnp.bfloat16)
    upstream = d_hidden.astype(jnp.float32)
    grad_gate = upstream * up_pre * gate_sig * (1.0 + gate_pre * (1.0 - gate_sig))
    grad_up = upstream * gate_act
    grad_pre = (
        jnp.stack([grad_gate, grad_up], axis=1).astype(jnp.bfloat16).reshape(slots, 2 * columns)
    )
    shard_piece = lax.all_gather(grad_pre, "row", axis=0, tiled=True)
    groups = shard_piece.shape[0] // slots
    slot_part = lax.slice_in_dim(slot_cols, 0, shard_piece.shape[0], axis=0).reshape(
        groups, slots, rows_local
    )
    block_terms = jnp.einsum(
        "gsd,gsf->gdf",
        slot_part,
        shard_piece.reshape(groups, slots, 2 * columns),
        preferred_element_type=jnp.float32,
    )
    rounded = lax.optimization_barrier(block_terms.astype(jnp.bfloat16)).astype(jnp.float32)
    grad_full = jnp.sum(rounded, axis=0)
    grad_blocks = grad_full.reshape(rows_local // BLK, BLK, 2, columns)
    block_max = lax.pmax(jnp.max(jnp.abs(grad_blocks), axis=(1, 3)), "col")
    update = (grad_blocks / (block_max[:, None, :, None] + epsilon)).reshape(rows_local, 2, columns)
    new_master = w_master - learn_rate * colmax * update
    return (hidden, update, new_master)


LANE = 128
SUB = 8
CUT = (1, 2)
FIRST = 3
SWAP = 1
SHARE = 4


def moved(src, dst, send, recv, to):
    return pltpu.make_async_remote_copy(
        src_ref=src,
        dst_ref=dst,
        send_sem=send,
        recv_sem=recv,
        device_id=to,
        device_id_type=pl.DeviceIdType.MESH,
    )


def wide_part(slots):
    return slots - slots * CUT[0] // CUT[1] // 16 * 16


def flipped(index, bit):
    return index + bit - 2 * bit * lax.rem(index // bit, 2)


def layer_kernel(
    routes_hbm, dh_hbm, tok_hbm, w_hbm, hid, grad_ref, cm_ref, inv_ref, wv,
    routes, dh, tokv, tokq, psendt, qsend, sc, turned, folded, cmx, wq,
    esend, erec, own, lsend, lrec, keep, xsend, xrec, ga, tops, flat, bmx,
    in_sem, tok_sem, w_sem, pt_send, pt_recv, y_send, y_recv, x_send, x_recv, z_send, z_recv,
    c_send, c_recv, b_send, b_recv, l_send, l_recv, xs_send, xs_recv,
    ga_send, ga_recv, gp_send, gp_recv, gf_send, gf_recv, e_send, e_recv,
):
    me = lax.axis_index("row")
    col = lax.axis_index("col")
    core = lax.rem(me, 2)
    partner = me + 1 - 2 * core
    across = lax.rem(me + 2, 4)
    diag = lax.rem(partner + 2, 4)
    group = bmx.shape[0]
    col_x = flipped(col, 1)
    col_z = flipped(col, 2)
    col_far = flipped(col, 4)
    quarter_of = lax.rem(col, 4)
    tiles = ga.shape[0]
    slots = hid.shape[0]
    rows = sc.shape[1]
    toks = routes.shape[1]
    chunks = w_sem.shape[1]
    piece = rows // chunks
    quarter = rows // 4
    sizes = (slots - wide_part(slots), wide_part(slots))
    starts = (0, sizes[0])
    bases = (2 * slots, 2 * slots + 2 * sizes[0])

    in_copies = (
        pltpu.make_async_copy(routes_hbm, routes, in_sem.at[0]),
        pltpu.make_async_copy(dh_hbm, dh, in_sem.at[1]),
    )
    in_copies[0].start()
    q_copies = []
    for n in range(4):
        q = (quarter_of, 3 - quarter_of)[n // 2]
        cols = pl.ds(pl.multiple_of((across, diag)[n % 2] * rows + q * quarter, LANE), quarter)
        q_copies.append(pltpu.make_async_copy(tok_hbm.at[:, cols], tokq.at[n], tok_sem.at[n]))
        q_copies[-1].start()
    tok_copies = []
    for n in range(2):
        cols = pl.ds(pl.multiple_of((partner, me)[n] * rows, LANE), rows)
        tok_copies.append(pltpu.make_async_copy(tok_hbm.at[:, cols], tokv.at[n], tok_sem.at[4 + n]))
        tok_copies[-1].start()
    w_copies = []
    for k in range(chunks):
        part = pl.ds(k * piece, piece)
        for p in range(2):
            w_copies.append(
                pltpu.make_async_copy(w_hbm.at[part, p, :], wv.at[p, part], w_sem.at[p, k])
            )
    in_copies[1].start()

    barrier = pltpu.get_barrier_semaphore()
    greeted = [{"row": r} for r in (across, diag, partner)] + [{"col": c} for c in (col_x, col_z, col_far)]
    for device in greeted:
        pl.semaphore_signal(barrier, inc=1, device_id=device, device_id_type=pl.DeviceIdType.MESH)

    before = lax.broadcasted_iota(jnp.int32, (LANE, LANE), 0)
    after = lax.broadcasted_iota(jnp.int32, (LANE, LANE), 1)
    ladder = jnp.where(before < after, 1.0, 0.0).astype(jnp.bfloat16)
    every = jnp.ones((LANE, LANE), jnp.bfloat16)
    in_copies[0].wait()
    for copy in w_copies:
        copy.start()
    named = jnp.logical_or(routes[0:1, :] == 0, routes[1:2, :] == 0)
    flag = jnp.where(named, 1.0, 0.0)
    mask = jnp.broadcast_to(flag, (16, toks)).astype(jnp.bfloat16)
    earlier = jnp.zeros((16, LANE), jnp.float32)
    places = []
    for k in range(toks // LANE):
        part = mask[:, k * LANE : (k + 1) * LANE]
        places.append(earlier + jnp.dot(part, ladder, preferred_element_type=jnp.float32))
        earlier = earlier + jnp.dot(part, every, preferred_element_type=jnp.float32)
    place = jnp.concatenate(places, axis=1)[0:1, :].astype(jnp.int32)
    slot_id = lax.broadcasted_iota(jnp.int32, (slots, toks), 0)
    pick = jnp.where(slot_id == place, flag, 0.0).astype(jnp.bfloat16)
    pl.semaphore_wait(barrier, len(greeted))

    def routed(h, jj, q):
        return sc.at[
            pl.ds(bases[h] + jj * sizes[h], sizes[h]),
            pl.ds(pl.multiple_of(q * quarter, LANE), quarter),
        ]

    def y_copy(h, n):
        return moved(
            qsend.at[n, pl.ds(starts[h], sizes[h])],
            routed(h, n % 2, (quarter_of, 3 - quarter_of)[n // 2]),
            y_send.at[4 * h + n],
            y_recv.at[4 * h + n],
            {"row": (across, diag)[n % 2]},
        )

    for n in range(4):
        q_copies[n].wait()
        many = slots if n < 2 else sizes[0]
        qsend[n, 0:many] = jnp.dot(pick[0:many], tokq[n], preferred_element_type=jnp.float32).astype(jnp.bfloat16)
        y_copy(0, n).start()
    def side_copies(h, jj):
        here = routed(h, jj, quarter_of)
        n = 2 * h + jj
        return (
            moved(here, here, x_send.at[n], x_recv.at[n], {"col": col_x}),
            moved(here, here, z_send.at[n], z_recv.at[n], {"col": col_z}),
        )

    def pass_on(h, jj):
        y_copy(h, jj).wait_recv()
        for copy in side_copies(h, jj):
            copy.start()

    def relay_x():
        block = routed(1, 1, lax.rem(col_z, 4))
        return moved(block, block, x_send.at[4], x_recv.at[4], {"col": col_x})

    def relay_z():
        block = routed(1, 0, lax.rem(col_x, 4))
        return moved(block, block, z_send.at[4], z_recv.at[4], {"col": col_z})

    def arrived_first():
        for jj in range(2):
            y_copy(0, 2 + jj).wait_recv()
            for copy in side_copies(0, jj):
                copy.wait_recv()

    def arrived_second():
        side_copies(1, 1)[0].wait_recv()
        side_copies(1, 0)[1].wait_recv()
        relay_z().wait_recv()
        relay_x().wait_recv()

    folded[...] = jnp.zeros(folded.shape, jnp.float32)

    def fold_chunk(k):
        for p in range(2):
            w_copies[2 * k + p].wait()

        def fold(t, carry):
            cols = pl.ds(pl.multiple_of(t * LANE, LANE), LANE)
            for p in range(2):
                tile = jnp.abs(wv[p, k * piece : (k + 1) * piece, cols])
                best = jnp.max(tile.reshape(-1, SUB, LANE), axis=0)
                folded[p, :, cols] = jnp.maximum(folded[p, :, cols], best)
            return carry

        lax.fori_loop(0, tiles, fold, 0)

    tok_copies[0].wait()
    psendt[...] = jnp.dot(pick, tokv[0], preferred_element_type=jnp.float32).astype(jnp.bfloat16)
    t_copy = moved(psendt, sc.at[pl.ds(slots, slots)], pt_send.at[0], pt_recv.at[0], {"row": partner})
    t_copy.start()
    tok_copies[1].wait()
    sc[0:slots, :] = jnp.dot(pick, tokv[1], preferred_element_type=jnp.float32).astype(jnp.bfloat16)
    pass_on(0, 0)
    fold_chunk(0)
    fold_chunk(1)
    turned[:, 0:slots] = sc[0:slots, :].T
    pass_on(0, 1)
    for k in range(2, chunks):
        fold_chunk(k)
    for p in range(2):
        cmx[0, p : p + 1, :] = jnp.max(folded[p], axis=0, keepdims=True)
    c_copies = []
    for j, row in enumerate((across, diag, partner)):
        c_copies.append(moved(cmx.at[0], cmx.at[j + 1], c_send.at[j], c_recv.at[j], {"row": row}))
        c_copies[-1].start()
    for n in range(2):
        y_copy(1, n).start()
    t_copy.wait()
    turned[:, slots : 2 * slots] = sc[slots : 2 * slots, :].T
    tops[...] = jnp.zeros(tops.shape, jnp.float32)
    in_copies[1].wait()
    for copy in c_copies:
        copy.wait()
    cm_ref[...] = jnp.maximum(jnp.maximum(cmx[0], cmx[1]), jnp.maximum(cmx[2], cmx[3]))
    arrived_first()

    def scale_row(t, p):
        cols = pl.ds(pl.multiple_of(t * LANE, LANE), LANE)
        return (cm_ref[p : p + 1, cols] + epsilon) / quant_range

    def swap_late(h, t):
        n, some = h * tiles + t, pl.ds(0, sizes[h])
        return moved(lsend.at[n, some], lrec.at[n, some], l_send.at[n], l_recv.at[n], {"row": partner})

    def swap_early(t):
        return moved(esend.at[t], erec.at[t], e_send.at[t], e_recv.at[t], {"row": partner})

    def cross(h, t):
        n, some = h * tiles + t, pl.ds(0, sizes[h])
        return moved(xsend.at[n, some], xrec.at[n, some], xs_send.at[n], xs_recv.at[n], {"row": across})

    def grad_block(h, t, j):
        return ga.at[t, pl.ds(j * slots + starts[h], sizes[h])]

    def share_across(h, t):
        n = h * tiles + t
        return moved(grad_block(h, t, 0), grad_block(h, t, 2), ga_send.at[n], ga_recv.at[n], {"row": across})

    def share_partner(h, t):
        n = h * tiles + t
        return moved(grad_block(h, t, 0), grad_block(h, t, 1), gp_send.at[n], gp_recv.at[n], {"row": partner})

    def forward(h, t):
        n = h * tiles + t
        return moved(grad_block(h, t, 2), grad_block(h, t, 3), gf_send.at[n], gf_recv.at[n], {"row": partner})

    def offer(h, t, term):
        n, size = h * tiles + t, sizes[h]
        lsend[n, 0:size] = term[size:].astype(jnp.bfloat16)
        swap_late(h, t).start()
        keep[lax.rem(n, SWAP + 1), 0:size] = term[:size]

    def cross_late(h, t):
        n, size = h * tiles + t, sizes[h]
        swap_late(h, t).wait_recv()
        both = keep[lax.rem(n, SWAP + 1), 0:size] + lrec[n, 0:size].astype(jnp.float32)
        xsend[n, 0:size] = both.astype(jnp.bfloat16)
        cross(h, t).start()

    def finalize(h, t):
        mine = slice(starts[h], starts[h] + sizes[h])
        cross(h, t).wait_recv()
        others = xrec[h * tiles + t, 0 : sizes[h]].astype(jnp.float32)
        total = own[t, mine] + erec[t, mine].astype(jnp.float32) + others
        gate_pre = total[:, :LANE] * scale_row(t, 0)
        up_pre = total[:, LANE:] * scale_row(t, 1)
        gate_sig = jax.nn.sigmoid(gate_pre)
        gate_act = gate_pre * gate_sig
        cols = pl.ds(pl.multiple_of(t * LANE, LANE), LANE)
        hid[mine, cols] = (gate_act * up_pre).astype(jnp.bfloat16)
        upstream = dh[mine, cols].astype(jnp.float32)
        grad_gate = upstream * up_pre * gate_sig * (1.0 + gate_pre * (1.0 - gate_sig))
        grad_up = upstream * gate_act
        ga[t, mine, :] = jnp.concatenate([grad_gate, grad_up], axis=1).astype(jnp.bfloat16)
        share_across(h, t).start()
        share_partner(h, t).start()

    def hand_over(h, t):
        share_across(h, t).wait_recv()
        forward(h, t).start()

    depth = 3 * BLK
    first_final = SWAP + FIRST
    second = tiles + 1
    second_final = second + tiles + SWAP
    second_share = second_final + SHARE
    last = second_share + 1 + tiles

    def during(i, start):
        return jnp.logical_and(i >= start, i < start + tiles)

    def step(i, carry):
        @pl.when(i == 2)
        def _():
            pass_on(1, 0)

        @pl.when(i == 3)
        def _():
            pass_on(1, 1)

        @pl.when(i == 5)
        def _():
            side_copies(1, 0)[0].wait_recv()
            relay_z().start()

        @pl.when(i == 7)
        def _():
            side_copies(1, 1)[1].wait_recv()
            relay_x().start()

        @pl.when(i < tiles)
        def _():
            for p in range(2):
                w = wv[p, :, pl.ds(pl.multiple_of(i * LANE, LANE), LANE)]
                wq[i, :, p * LANE : (p + 1) * LANE] = (w * (1.0 / scale_row(i, p))).astype(jnp.bfloat16)
            term = jnp.dot(sc[0 : bases[1], :], wq[i], preferred_element_type=jnp.float32)
            offer(0, i, term[2 * slots :])
            esend[i] = term[slots : 2 * slots].astype(jnp.bfloat16)
            swap_early(i).start()
            own[i] = term[:slots]

        @pl.when(during(i, SWAP))
        def _():
            cross_late(0, i - SWAP)

        @pl.when(during(i, first_final))
        def _():
            t = i - first_final
            swap_early(t).wait_recv()
            finalize(0, t)

        @pl.when(i == second)
        def _():
            arrived_second()

        @pl.when(during(i, second))
        def _():
            t = i - second
            offer(1, t, jnp.dot(sc[bases[1] :, :], wq[t], preferred_element_type=jnp.float32))

        @pl.when(during(i, second + SWAP))
        def _():
            cross_late(1, i - second - SWAP)

        @pl.when(i == second + 1)
        def _():
            for jj in range(2):
                block = [sc[bases[h] + jj * sizes[h] : bases[h] + (jj + 1) * sizes[h], :] for h in range(2)]
                turned[:, (2 + jj) * slots : (3 + jj) * slots] = jnp.concatenate(block, axis=0).T

        @pl.when(during(i, second + SWAP))
        def _():
            hand_over(0, i - second - SWAP)

        @pl.when(during(i, second_final))
        def _():
            finalize(1, i - second_final)

        @pl.when(during(i, second_share))
        def _():
            hand_over(1, i - second_share)

        @pl.when(i >= second_share + 1)
        def _():
            t = i - second_share - 1
            for h in range(2):
                share_partner(h, t).wait_recv()
                forward(h, t).wait_recv()
            cols = pl.ds(pl.multiple_of(t * 2 * LANE, 2 * LANE), 2 * LANE)
            for k in range(rows // depth):
                grad = jnp.dot(turned[k * depth : (k + 1) * depth, :], ga[t], preferred_element_type=jnp.float32)
                grad_ref[k * depth : (k + 1) * depth, cols] = grad.astype(jnp.bfloat16)
                for b in range(3):
                    for p in range(2):
                        n = 2 * (3 * k + b) + p
                        tile = jnp.abs(grad[b * BLK : (b + 1) * BLK, p * LANE : (p + 1) * LANE])
                        tops[n] = jnp.maximum(tops[n], jnp.max(tile.reshape(-1, SUB, LANE), axis=0))

        return carry

    lax.fori_loop(0, last, step, 0)

    for n in range(tops.shape[0]):
        flat[n : n + 1, :] = jnp.max(tops[n], axis=0, keepdims=True)
    lane = lax.broadcasted_iota(jnp.int32, (SUB, LANE), 1)
    packs = tops.shape[0] // SUB
    packed = jnp.zeros((SUB, LANE), jnp.float32)
    for k in range(packs):
        widest = jnp.max(flat[k * SUB : (k + 1) * SUB, :], axis=1, keepdims=True)
        packed = jnp.where(lane == k, widest, packed)
    bmx[0] = packed
    b_copies = []
    for k in range(1, group):
        b_copies.append(
            moved(bmx.at[0], bmx.at[k], b_send.at[k - 1], b_recv.at[k - 1], {"col": lax.rem(col + k, group)})
        )
        b_copies[-1].start()

    def finish(t, carry):
        swap_early(t).wait_send()
        for h in range(2):
            for copy in (swap_late, cross, share_across, share_partner, forward):
                copy(h, t).wait_send()
        return carry

    lax.fori_loop(0, tiles, finish, 0)
    relay_x().wait_send()
    relay_z().wait_send()
    for h in range(2):
        for n in range(4 - 2 * h):
            y_copy(h, n).wait_send()
        for jj in range(2):
            for copy in side_copies(h, jj):
                copy.wait_send()
    for copy in b_copies:
        copy.wait()
    best = bmx[0]
    for k in range(1, group):
        best = jnp.maximum(best, bmx[k])
    for k in range(packs):
        block_max = jnp.max(jnp.where(lane == k, best, 0.0), axis=1, keepdims=True)
        inv_ref[k * SUB : (k + 1) * SUB, :] = jnp.broadcast_to(1.0 / (block_max + epsilon), (SUB, LANE))


def update_kernel(inv_ref, cm_ref, grad_ref, hid, wv, out_hbm, update_hbm, new_hbm, uv, nv, u_sem, n_sem, h_sem):
    blocks = u_sem.shape[1]
    columns = wv.shape[2]
    tiles = columns // LANE

    def part(b):
        return pl.ds(pl.multiple_of(b * BLK, BLK), BLK)

    def put_update(b, p):
        return pltpu.make_async_copy(uv.at[p, part(b)], update_hbm.at[part(b), p, :], u_sem.at[p, b])

    def put_new(b, p):
        return pltpu.make_async_copy(nv.at[p, part(b)], new_hbm.at[part(b), p, :], n_sem.at[p, b])

    def step(b, carry):
        for p in range(2):
            inverse = inv_ref[pl.ds(2 * b + p, 1), :]
            for t in range(tiles):
                cols = slice(t * LANE, (t + 1) * LANE)
                at = (2 * t + p) * LANE
                update = grad_ref[part(b), at : at + LANE].astype(jnp.float32) * inverse
                uv[p, part(b), cols] = update
                nv[p, part(b), cols] = wv[p, part(b), cols] - (learn_rate * cm_ref[p : p + 1, cols]) * update
            put_update(b, p).start()
            put_new(b, p).start()
        return carry

    def finish(b, carry):
        for p in range(2):
            put_update(b, p).wait()
            put_new(b, p).wait()
        return carry

    put_hidden = pltpu.make_async_copy(hid, out_hbm, h_sem.at[0])
    put_hidden.start()
    lax.fori_loop(0, blocks, step, 0)
    lax.fori_loop(0, blocks, finish, 0)
    put_hidden.wait()


def on_device(tokens, routes, w_master, d_hidden):
    rows, _, columns = w_master.shape
    slots = d_hidden.shape[0]
    toks = tokens.shape[0]
    aligned = columns % LANE == 0 and rows % (12 * BLK) == 0 and slots % 32 == 0 and toks % LANE == 0
    aligned = aligned and 2 * rows // BLK <= SUB * LANE
    if lax.axis_size("row") != 4 or lax.axis_size("col") != 8 or not aligned:
        return on_device_plain(tokens, routes, w_master, d_hidden)
    group = lax.axis_size("col")
    tiles = columns // LANE
    bf16, f32 = jnp.bfloat16, jnp.float32
    chunks = 6
    blocks = rows // BLK
    vmem = pl.BlockSpec(memory_space=pltpu.VMEM)
    hbm = pl.BlockSpec(memory_space=pltpu.HBM)
    dma = pltpu.SemaphoreType.DMA
    wide = 2 * LANE
    hidden, grad, colmax, inverse, master = pl.pallas_call(
        layer_kernel,
        name="layer_exchange",
        out_shape=(
            pltpu.VMEM((slots, columns), bf16),
            pltpu.VMEM((rows, 2 * columns), bf16),
            pltpu.VMEM((2, columns), f32),
            pltpu.VMEM((2 * blocks, LANE), f32),
            pltpu.VMEM((2, rows, columns), f32),
        ),
        in_specs=[hbm, hbm, hbm, hbm],
        out_specs=(vmem,) * 5,
        scratch_shapes=[
            pltpu.VMEM((2, toks), jnp.int32),
            pltpu.VMEM((slots, columns), bf16),
            pltpu.VMEM((2, toks, rows), bf16),
            pltpu.VMEM((4, toks, rows // 4), bf16),
            pltpu.VMEM((slots, rows), bf16),
            pltpu.VMEM((4, slots, rows // 4), bf16),
            pltpu.VMEM((4 * slots, rows), bf16),
            pltpu.VMEM((rows, 4 * slots), bf16),
            pltpu.VMEM((2, SUB, columns), f32),
            pltpu.VMEM((4, 2, columns), f32),
            pltpu.VMEM((tiles, rows, wide), bf16),
            pltpu.VMEM((tiles, slots, wide), bf16),
            pltpu.VMEM((tiles, slots, wide), bf16),
            pltpu.VMEM((tiles, slots, wide), f32),
            pltpu.VMEM((2 * tiles, wide_part(slots), wide), bf16),
            pltpu.VMEM((2 * tiles, wide_part(slots), wide), bf16),
            pltpu.VMEM((SWAP + 1, wide_part(slots), wide), f32),
            pltpu.VMEM((2 * tiles, wide_part(slots), wide), bf16),
            pltpu.VMEM((2 * tiles, wide_part(slots), wide), bf16),
            pltpu.VMEM((tiles, 4 * slots, wide), bf16),
            pltpu.VMEM((2 * blocks, SUB, LANE), f32),
            pltpu.VMEM((2 * blocks, LANE), f32),
            pltpu.VMEM((group, SUB, LANE), f32),
            dma((2,)),
            dma((6,)),
            dma((2, chunks)),
            dma((1,)),
            dma((1,)),
            dma((6,)),
            dma((6,)),
        ]
        + [dma((5,))] * 4
        + [dma((3,))] * 2
        + [dma((group - 1,))] * 2
        + [dma((2 * tiles,))] * 10
        + [dma((tiles,))] * 2,
        compiler_params=pltpu.CompilerParams(
            collective_id=0, has_side_effects=True, vmem_limit_bytes=34 * 1024 * 1024
        ),
    )(*(pltpu.with_memory_space_constraint(x, pltpu.HBM) for x in (routes.T, d_hidden, tokens, w_master)))
    hidden, update, new_master = pl.pallas_call(
        update_kernel,
        name="master_update",
        out_shape=(jax.ShapeDtypeStruct((slots, columns), bf16),)
        + (jax.ShapeDtypeStruct(w_master.shape, f32),) * 2,
        in_specs=[vmem] * 5,
        out_specs=(hbm, hbm, hbm),
        scratch_shapes=[
            pltpu.VMEM((2, rows, columns), f32),
            pltpu.VMEM((2, rows, columns), f32),
            dma((2, blocks)),
            dma((2, blocks)),
            dma((1,)),
        ],
        compiler_params=pltpu.CompilerParams(vmem_limit_bytes=30 * 1024 * 1024),
    )(inverse, colmax, grad, hidden, master)
    return (hidden, update, new_master)


def solution(mesh):
    in_specs = (P("row", None), P("row", None), P("row", None, "col"), P("row", "col"))
    out_specs = (P("row", "col"), P("row", None, "col"), P("row", None, "col"))
    return jax.shard_map(
        on_device, mesh=mesh, in_specs=in_specs, out_specs=out_specs, check_vma=False
    )
```

```python
import jax
import jax.numpy as jnp
from jax import lax
from jax.experimental import pallas as pl
from jax.experimental.pallas import tpu as pltpu
from jax.sharding import PartitionSpec as P

BLK = 128


epsilon = 1e-06
quant_range = 448.0
learn_rate = 0.05


def on_device_plain(tokens, routes, w_master, d_hidden):
    rows_local, _, columns = w_master.shape
    slots = d_hidden.shape[0]
    colmax = lax.pmax(jnp.max(jnp.abs(w_master), axis=0), "row")
    wscale = (colmax + epsilon) / quant_range
    quantized = (w_master / wscale).astype(jnp.bfloat16).reshape(rows_local, 2 * columns)
    flat_scale = wscale.reshape(2 * columns)
    routed = jnp.any(routes == 0, axis=1)
    picked = jnp.nonzero(routed, size=slots)[0].astype(jnp.int32)
    slot_rows = tokens[picked]
    slot_cols = lax.all_to_all(slot_rows, "row", split_axis=1, concat_axis=0, tiled=True)
    slot_part = lax.slice_in_dim(slot_cols, 0, lax.axis_size("row") * slots, axis=0)
    summed = lax.psum_scatter(
        jnp.dot(slot_part, quantized, preferred_element_type=jnp.float32).astype(jnp.bfloat16),
        "row",
        scatter_dimension=0,
        tiled=True,
    ).astype(jnp.float32)
    projected = (summed * flat_scale).reshape(slots, 2, columns)
    gate_pre = projected[:, 0]
    up_pre = projected[:, 1]
    gate_sig = jax.nn.sigmoid(gate_pre)
    gate_act = gate_pre * gate_sig
    hidden = (gate_act * up_pre).astype(jnp.bfloat16)
    upstream = d_hidden.astype(jnp.float32)
    grad_gate = upstream * up_pre * gate_sig * (1.0 + gate_pre * (1.0 - gate_sig))
    grad_up = upstream * gate_act
    grad_pre = (
        jnp.stack([grad_gate, grad_up], axis=1).astype(jnp.bfloat16).reshape(slots, 2 * columns)
    )
    shard_piece = lax.all_gather(grad_pre, "row", axis=0, tiled=True)
    groups = shard_piece.shape[0] // slots
    slot_part = lax.slice_in_dim(slot_cols, 0, shard_piece.shape[0], axis=0).reshape(
        groups, slots, rows_local
    )
    block_terms = jnp.einsum(
        "gsd,gsf->gdf",
        slot_part,
        shard_piece.reshape(groups, slots, 2 * columns),
        preferred_element_type=jnp.float32,
    )
    rounded = lax.optimization_barrier(block_terms.astype(jnp.bfloat16)).astype(jnp.float32)
    grad_full = jnp.sum(rounded, axis=0)
    grad_blocks = grad_full.reshape(rows_local // BLK, BLK, 2, columns)
    block_max = lax.pmax(jnp.max(jnp.abs(grad_blocks), axis=(1, 3)), "col")
    update = (grad_blocks / (block_max[:, None, :, None] + epsilon)).reshape(rows_local, 2, columns)
    new_master = w_master - learn_rate * colmax * update
    return (hidden, update, new_master)


LANE = 128
SUB = 8
CUT = (1, 2)
FIRST = 3
SWAP = 1
SHARE = 4


def moved(src, dst, send, recv, to):
    return pltpu.make_async_remote_copy(
        src_ref=src,
        dst_ref=dst,
        send_sem=send,
        recv_sem=recv,
        device_id=to,
        device_id_type=pl.DeviceIdType.MESH,
    )


def wide_part(slots):
    return slots - slots * CUT[0] // CUT[1] // 16 * 16


def flipped(index, bit):
    return index + bit - 2 * bit * lax.rem(index // bit, 2)


def layer_kernel(
    routes_hbm, dh_hbm, tok_hbm, w_hbm, hid, grad_ref, cm_ref, inv_ref, wv,
    routes, dh, tokv, tokq, psendt, qsend, sc, turned, folded, cmx, wq,
    esend, erec, own, lsend, lrec, keep, xsend, xrec, ga, tops, flat, bmx,
    in_sem, tok_sem, w_sem, pt_send, pt_recv, y_send, y_recv, x_send, x_recv, z_send, z_recv,
    c_send, c_recv, b_send, b_recv, l_send, l_recv, xs_send, xs_recv,
    ga_send, ga_recv, gp_send, gp_recv, gf_send, gf_recv, e_send, e_recv,
):
    me = lax.axis_index("row")
    col = lax.axis_index("col")
    core = lax.rem(me, 2)
    partner = me + 1 - 2 * core
    across = lax.rem(me + 2, 4)
    diag = lax.rem(partner + 2, 4)
    group = bmx.shape[0]
    col_x = flipped(col, 1)
    col_z = flipped(col, 2)
    col_far = flipped(col, 4)
    quarter_of = lax.rem(col, 4)
    tiles = ga.shape[0]
    slots = hid.shape[0]
    rows = sc.shape[1]
    toks = routes.shape[1]
    chunks = w_sem.shape[1]
    piece = rows // chunks
    quarter = rows // 4
    sizes = (slots - wide_part(slots), wide_part(slots))
    starts = (0, sizes[0])
    bases = (2 * slots, 2 * slots + 2 * sizes[0])

    in_copies = (
        pltpu.make_async_copy(routes_hbm, routes, in_sem.at[0]),
        pltpu.make_async_copy(dh_hbm, dh, in_sem.at[1]),
    )
    in_copies[0].start()
    q_copies = []
    for n in range(4):
        q = (quarter_of, 3 - quarter_of)[n // 2]
        cols = pl.ds(pl.multiple_of((across, diag)[n % 2] * rows + q * quarter, LANE), quarter)
        q_copies.append(pltpu.make_async_copy(tok_hbm.at[:, cols], tokq.at[n], tok_sem.at[n]))
        q_copies[-1].start()
    tok_copies = []
    for n in range(2):
        cols = pl.ds(pl.multiple_of((partner, me)[n] * rows, LANE), rows)
        tok_copies.append(pltpu.make_async_copy(tok_hbm.at[:, cols], tokv.at[n], tok_sem.at[4 + n]))
        tok_copies[-1].start()
    w_copies = []
    for k in range(chunks):
        part = pl.ds(k * piece, piece)
        for p in range(2):
            w_copies.append(
                pltpu.make_async_copy(w_hbm.at[part, p, :], wv.at[p, part], w_sem.at[p, k])
            )
    in_copies[1].start()

    barrier = pltpu.get_barrier_semaphore()
    greeted = [{"row": r} for r in (across, diag, partner)] + [{"col": c} for c in (col_x, col_z, col_far)]
    for device in greeted:
        pl.semaphore_signal(barrier, inc=1, device_id=device, device_id_type=pl.DeviceIdType.MESH)

    before = lax.broadcasted_iota(jnp.int32, (LANE, LANE), 0)
    after = lax.broadcasted_iota(jnp.int32, (LANE, LANE), 1)
    ladder = jnp.where(before < after, 1.0, 0.0).astype(jnp.bfloat16)
    every = jnp.ones((LANE, LANE), jnp.bfloat16)
    in_copies[0].wait()
    for copy in w_copies:
        copy.start()
    named = jnp.logical_or(routes[0:1, :] == 0, routes[1:2, :] == 0)
    flag = jnp.where(named, 1.0, 0.0)
    mask = jnp.broadcast_to(flag, (16, toks)).astype(jnp.bfloat16)
    earlier = jnp.zeros((16, LANE), jnp.float32)
    places = []
    for k in range(toks // LANE):
        part = mask[:, k * LANE : (k + 1) * LANE]
        places.append(earlier + jnp.dot(part, ladder, preferred_element_type=jnp.float32))
        earlier = earlier + jnp.dot(part, every, preferred_element_type=jnp.float32)
    place = jnp.concatenate(places, axis=1)[0:1, :].astype(jnp.int32)
    slot_id = lax.broadcasted_iota(jnp.int32, (slots, toks), 0)
    pick = jnp.where(slot_id == place, flag, 0.0).astype(jnp.bfloat16)

    def routed(h, jj, q):
        return sc.at[
            pl.ds(bases[h] + jj * sizes[h], sizes[h]),
            pl.ds(pl.multiple_of(q * quarter, LANE), quarter),
        ]

    def y_copy(h, n):
        return moved(
            qsend.at[n, pl.ds(starts[h], sizes[h])],
            routed(h, n % 2, (quarter_of, 3 - quarter_of)[n // 2]),
            y_send.at[4 * h + n],
            y_recv.at[4 * h + n],
            {"row": (across, diag)[n % 2]},
        )

    for n in range(4):
        q_copies[n].wait()
        many = slots if n < 2 else sizes[0]
        qsend[n, 0:many] = jnp.dot(pick[0:many], tokq[n], preferred_element_type=jnp.float32).astype(jnp.bfloat16)
        if n == 0:
            pl.semaphore_wait(barrier, len(greeted))
        y_copy(0, n).start()
    def side_copies(h, jj):
        here = routed(h, jj, quarter_of)
        n = 2 * h + jj
        return (
            moved(here, here, x_send.at[n], x_recv.at[n], {"col": col_x}),
            moved(here, here, z_send.at[n], z_recv.at[n], {"col": col_z}),
        )

    def pass_on(h, jj):
        y_copy(h, jj).wait_recv()
        for copy in side_copies(h, jj):
            copy.start()

    def relay_x():
        block = routed(1, 1, lax.rem(col_z, 4))
        return moved(block, block, x_send.at[4], x_recv.at[4], {"col": col_x})

    def relay_z():
        block = routed(1, 0, lax.rem(col_x, 4))
        return moved(block, block, z_send.at[4], z_recv.at[4], {"col": col_z})

    def arrived_first():
        for jj in range(2):
            y_copy(0, 2 + jj).wait_recv()
            for copy in side_copies(0, jj):
                copy.wait_recv()

    def arrived_second():
        side_copies(1, 1)[0].wait_recv()
        side_copies(1, 0)[1].wait_recv()
        relay_z().wait_recv()
        relay_x().wait_recv()

    folded[...] = jnp.zeros(folded.shape, jnp.float32)

    def fold_chunk(k):
        for p in range(2):
            w_copies[2 * k + p].wait()

        def fold(t, carry):
            cols = pl.ds(pl.multiple_of(t * LANE, LANE), LANE)
            for p in range(2):
                tile = jnp.abs(wv[p, k * piece : (k + 1) * piece, cols])
                best = jnp.max(tile.reshape(-1, SUB, LANE), axis=0)
                folded[p, :, cols] = jnp.maximum(folded[p, :, cols], best)
            return carry

        lax.fori_loop(0, tiles, fold, 0)

    tok_copies[0].wait()
    psendt[...] = jnp.dot(pick, tokv[0], preferred_element_type=jnp.float32).astype(jnp.bfloat16)
    t_copy = moved(psendt, sc.at[pl.ds(slots, slots)], pt_send.at[0], pt_recv.at[0], {"row": partner})
    t_copy.start()
    tok_copies[1].wait()
    sc[0:slots, :] = jnp.dot(pick, tokv[1], preferred_element_type=jnp.float32).astype(jnp.bfloat16)
    pass_on(0, 0)
    fold_chunk(0)
    fold_chunk(1)
    turned[:, 0:slots] = sc[0:slots, :].T
    pass_on(0, 1)
    for k in range(2, chunks):
        fold_chunk(k)
    for p in range(2):
        cmx[0, p : p + 1, :] = jnp.max(folded[p], axis=0, keepdims=True)
    c_copies = []
    for j, row in enumerate((across, diag, partner)):
        c_copies.append(moved(cmx.at[0], cmx.at[j + 1], c_send.at[j], c_recv.at[j], {"row": row}))
        c_copies[-1].start()
    for n in range(2):
        y_copy(1, n).start()
    t_copy.wait()
    turned[:, slots : 2 * slots] = sc[slots : 2 * slots, :].T
    tops[...] = jnp.zeros(tops.shape, jnp.float32)
    in_copies[1].wait()
    for copy in c_copies:
        copy.wait()
    cm_ref[...] = jnp.maximum(jnp.maximum(cmx[0], cmx[1]), jnp.maximum(cmx[2], cmx[3]))
    arrived_first()

    def scale_row(t, p):
        cols = pl.ds(pl.multiple_of(t * LANE, LANE), LANE)
        return (cm_ref[p : p + 1, cols] + epsilon) / quant_range

    def swap_late(h, t):
        n, some = h * tiles + t, pl.ds(0, sizes[h])
        return moved(lsend.at[n, some], lrec.at[n, some], l_send.at[n], l_recv.at[n], {"row": partner})

    def swap_early(t):
        return moved(esend.at[t], erec.at[t], e_send.at[t], e_recv.at[t], {"row": partner})

    def cross(h, t):
        n, some = h * tiles + t, pl.ds(0, sizes[h])
        return moved(xsend.at[n, some], xrec.at[n, some], xs_send.at[n], xs_recv.at[n], {"row": across})

    def grad_block(h, t, j):
        return ga.at[t, pl.ds(j * slots + starts[h], sizes[h])]

    def share_across(h, t):
        n = h * tiles + t
        return moved(grad_block(h, t, 0), grad_block(h, t, 2), ga_send.at[n], ga_recv.at[n], {"row": across})

    def share_partner(h, t):
        n = h * tiles + t
        return moved(grad_block(h, t, 0), grad_block(h, t, 1), gp_send.at[n], gp_recv.at[n], {"row": partner})

    def forward(h, t):
        n = h * tiles + t
        return moved(grad_block(h, t, 2), grad_block(h, t, 3), gf_send.at[n], gf_recv.at[n], {"row": partner})

    def offer(h, t, term):
        n, size = h * tiles + t, sizes[h]
        lsend[n, 0:size] = term[size:].astype(jnp.bfloat16)
        swap_late(h, t).start()
        keep[lax.rem(n, SWAP + 1), 0:size] = term[:size]

    def cross_late(h, t):
        n, size = h * tiles + t, sizes[h]
        swap_late(h, t).wait_recv()
        both = keep[lax.rem(n, SWAP + 1), 0:size] + lrec[n, 0:size].astype(jnp.float32)
        xsend[n, 0:size] = both.astype(jnp.bfloat16)
        cross(h, t).start()

    def finalize(h, t):
        mine = slice(starts[h], starts[h] + sizes[h])
        cross(h, t).wait_recv()
        others = xrec[h * tiles + t, 0 : sizes[h]].astype(jnp.float32)
        total = own[t, mine] + erec[t, mine].astype(jnp.float32) + others
        gate_pre = total[:, :LANE] * scale_row(t, 0)
        up_pre = total[:, LANE:] * scale_row(t, 1)
        gate_sig = jax.nn.sigmoid(gate_pre)
        gate_act = gate_pre * gate_sig
        cols = pl.ds(pl.multiple_of(t * LANE, LANE), LANE)
        hid[mine, cols] = (gate_act * up_pre).astype(jnp.bfloat16)
        upstream = dh[mine, cols].astype(jnp.float32)
        grad_gate = upstream * up_pre * gate_sig * (1.0 + gate_pre * (1.0 - gate_sig))
        grad_up = upstream * gate_act
        ga[t, mine, :] = jnp.concatenate([grad_gate, grad_up], axis=1).astype(jnp.bfloat16)
        share_across(h, t).start()
        share_partner(h, t).start()

    def hand_over(h, t):
        share_across(h, t).wait_recv()
        forward(h, t).start()

    depth = 3 * BLK
    first_final = SWAP + FIRST
    second = tiles + 1
    second_final = second + tiles + SWAP
    second_share = second_final + SHARE
    last = second_share + 1 + tiles

    def during(i, start):
        return jnp.logical_and(i >= start, i < start + tiles)

    def step(i, carry):
        @pl.when(i == 2)
        def _():
            pass_on(1, 0)

        @pl.when(i == 3)
        def _():
            pass_on(1, 1)

        @pl.when(i == 5)
        def _():
            side_copies(1, 0)[0].wait_recv()
            relay_z().start()

        @pl.when(i == 7)
        def _():
            side_copies(1, 1)[1].wait_recv()
            relay_x().start()

        @pl.when(i < tiles)
        def _():
            for p in range(2):
                w = wv[p, :, pl.ds(pl.multiple_of(i * LANE, LANE), LANE)]
                wq[i, :, p * LANE : (p + 1) * LANE] = (w * (1.0 / scale_row(i, p))).astype(jnp.bfloat16)
            term = jnp.dot(sc[0 : bases[1], :], wq[i], preferred_element_type=jnp.float32)
            offer(0, i, term[2 * slots :])
            esend[i] = term[slots : 2 * slots].astype(jnp.bfloat16)
            swap_early(i).start()
            own[i] = term[:slots]

        @pl.when(during(i, SWAP))
        def _():
            cross_late(0, i - SWAP)

        @pl.when(during(i, first_final))
        def _():
            t = i - first_final
            swap_early(t).wait_recv()
            finalize(0, t)

        @pl.when(i == second)
        def _():
            arrived_second()

        @pl.when(during(i, second))
        def _():
            t = i - second
            offer(1, t, jnp.dot(sc[bases[1] :, :], wq[t], preferred_element_type=jnp.float32))

        @pl.when(during(i, second + SWAP))
        def _():
            cross_late(1, i - second - SWAP)

        @pl.when(i == second + 1)
        def _():
            for jj in range(2):
                block = [sc[bases[h] + jj * sizes[h] : bases[h] + (jj + 1) * sizes[h], :] for h in range(2)]
                turned[:, (2 + jj) * slots : (3 + jj) * slots] = jnp.concatenate(block, axis=0).T

        @pl.when(during(i, second + SWAP))
        def _():
            hand_over(0, i - second - SWAP)

        @pl.when(during(i, second_final))
        def _():
            finalize(1, i - second_final)

        @pl.when(during(i, second_share))
        def _():
            hand_over(1, i - second_share)

        @pl.when(i >= second_share + 1)
        def _():
            t = i - second_share - 1
            for h in range(2):
                share_partner(h, t).wait_recv()
                forward(h, t).wait_recv()
            cols = pl.ds(pl.multiple_of(t * 2 * LANE, 2 * LANE), 2 * LANE)
            for k in range(rows // depth):
                grad = jnp.dot(turned[k * depth : (k + 1) * depth, :], ga[t], preferred_element_type=jnp.float32)
                grad_ref[k * depth : (k + 1) * depth, cols] = grad.astype(jnp.bfloat16)
                for b in range(3):
                    for p in range(2):
                        n = 2 * (3 * k + b) + p
                        tile = jnp.abs(grad[b * BLK : (b + 1) * BLK, p * LANE : (p + 1) * LANE])
                        tops[n] = jnp.maximum(tops[n], jnp.max(tile.reshape(-1, SUB, LANE), axis=0))

        return carry

    lax.fori_loop(0, last, step, 0)

    for n in range(tops.shape[0]):
        flat[n : n + 1, :] = jnp.max(tops[n], axis=0, keepdims=True)
    lane = lax.broadcasted_iota(jnp.int32, (SUB, LANE), 1)
    packs = tops.shape[0] // SUB
    packed = jnp.zeros((SUB, LANE), jnp.float32)
    for k in range(packs):
        widest = jnp.max(flat[k * SUB : (k + 1) * SUB, :], axis=1, keepdims=True)
        packed = jnp.where(lane == k, widest, packed)
    bmx[0] = packed
    b_copies = []
    for k in range(1, group):
        b_copies.append(
            moved(bmx.at[0], bmx.at[k], b_send.at[k - 1], b_recv.at[k - 1], {"col": lax.rem(col + k, group)})
        )
        b_copies[-1].start()

    def finish(t, carry):
        swap_early(t).wait_send()
        for h in range(2):
            for copy in (swap_late, cross, share_across, share_partner, forward):
                copy(h, t).wait_send()
        return carry

    lax.fori_loop(0, tiles, finish, 0)
    relay_x().wait_send()
    relay_z().wait_send()
    for h in range(2):
        for n in range(4 - 2 * h):
            y_copy(h, n).wait_send()
        for jj in range(2):
            for copy in side_copies(h, jj):
                copy.wait_send()
    for copy in b_copies:
        copy.wait()
    best = bmx[0]
    for k in range(1, group):
        best = jnp.maximum(best, bmx[k])
    for k in range(packs):
        block_max = jnp.max(jnp.where(lane == k, best, 0.0), axis=1, keepdims=True)
        inv_ref[k * SUB : (k + 1) * SUB, :] = jnp.broadcast_to(1.0 / (block_max + epsilon), (SUB, LANE))


def update_kernel(inv_ref, cm_ref, grad_ref, hid, wv, out_hbm, update_hbm, new_hbm, uv, nv, u_sem, n_sem, h_sem):
    blocks = u_sem.shape[1]
    columns = wv.shape[2]
    tiles = columns // LANE

    def part(b):
        return pl.ds(pl.multiple_of(b * BLK, BLK), BLK)

    def put_update(b, p):
        return pltpu.make_async_copy(uv.at[p, part(b)], update_hbm.at[part(b), p, :], u_sem.at[p, b])

    def put_new(b, p):
        return pltpu.make_async_copy(nv.at[p, part(b)], new_hbm.at[part(b), p, :], n_sem.at[p, b])

    def step(b, carry):
        for p in range(2):
            inverse = inv_ref[pl.ds(2 * b + p, 1), :]
            for t in range(tiles):
                cols = slice(t * LANE, (t + 1) * LANE)
                at = (2 * t + p) * LANE
                update = grad_ref[part(b), at : at + LANE].astype(jnp.float32) * inverse
                uv[p, part(b), cols] = update
                nv[p, part(b), cols] = wv[p, part(b), cols] - (learn_rate * cm_ref[p : p + 1, cols]) * update
            put_update(b, p).start()
            put_new(b, p).start()
        return carry

    def finish(b, carry):
        for p in range(2):
            put_update(b, p).wait()
            put_new(b, p).wait()
        return carry

    put_hidden = pltpu.make_async_copy(hid, out_hbm, h_sem.at[0])
    put_hidden.start()
    lax.fori_loop(0, blocks, step, 0)
    lax.fori_loop(0, blocks, finish, 0)
    put_hidden.wait()


def on_device(tokens, routes, w_master, d_hidden):
    rows, _, columns = w_master.shape
    slots = d_hidden.shape[0]
    toks = tokens.shape[0]
    aligned = columns % LANE == 0 and rows % (12 * BLK) == 0 and slots % 32 == 0 and toks % LANE == 0
    aligned = aligned and 2 * rows // BLK <= SUB * LANE
    if lax.axis_size("row") != 4 or lax.axis_size("col") != 8 or not aligned:
        return on_device_plain(tokens, routes, w_master, d_hidden)
    group = lax.axis_size("col")
    tiles = columns // LANE
    bf16, f32 = jnp.bfloat16, jnp.float32
    chunks = 6
    blocks = rows // BLK
    vmem = pl.BlockSpec(memory_space=pltpu.VMEM)
    hbm = pl.BlockSpec(memory_space=pltpu.HBM)
    dma = pltpu.SemaphoreType.DMA
    wide = 2 * LANE
    hidden, grad, colmax, inverse, master = pl.pallas_call(
        layer_kernel,
        name="layer_exchange",
        out_shape=(
            pltpu.VMEM((slots, columns), bf16),
            pltpu.VMEM((rows, 2 * columns), bf16),
            pltpu.VMEM((2, columns), f32),
            pltpu.VMEM((2 * blocks, LANE), f32),
            pltpu.VMEM((2, rows, columns), f32),
        ),
        in_specs=[hbm, hbm, hbm, hbm],
        out_specs=(vmem,) * 5,
        scratch_shapes=[
            pltpu.VMEM((2, toks), jnp.int32),
            pltpu.VMEM((slots, columns), bf16),
            pltpu.VMEM((2, toks, rows), bf16),
            pltpu.VMEM((4, toks, rows // 4), bf16),
            pltpu.VMEM((slots, rows), bf16),
            pltpu.VMEM((4, slots, rows // 4), bf16),
            pltpu.VMEM((4 * slots, rows), bf16),
            pltpu.VMEM((rows, 4 * slots), bf16),
            pltpu.VMEM((2, SUB, columns), f32),
            pltpu.VMEM((4, 2, columns), f32),
            pltpu.VMEM((tiles, rows, wide), bf16),
            pltpu.VMEM((tiles, slots, wide), bf16),
            pltpu.VMEM((tiles, slots, wide), bf16),
            pltpu.VMEM((tiles, slots, wide), f32),
            pltpu.VMEM((2 * tiles, wide_part(slots), wide), bf16),
            pltpu.VMEM((2 * tiles, wide_part(slots), wide), bf16),
            pltpu.VMEM((SWAP + 1, wide_part(slots), wide), f32),
            pltpu.VMEM((2 * tiles, wide_part(slots), wide), bf16),
            pltpu.VMEM((2 * tiles, wide_part(slots), wide), bf16),
            pltpu.VMEM((tiles, 4 * slots, wide), bf16),
            pltpu.VMEM((2 * blocks, SUB, LANE), f32),
            pltpu.VMEM((2 * blocks, LANE), f32),
            pltpu.VMEM((group, SUB, LANE), f32),
            dma((2,)),
            dma((6,)),
            dma((2, chunks)),
            dma((1,)),
            dma((1,)),
            dma((6,)),
            dma((6,)),
        ]
        + [dma((5,))] * 4
        + [dma((3,))] * 2
        + [dma((group - 1,))] * 2
        + [dma((2 * tiles,))] * 10
        + [dma((tiles,))] * 2,
        compiler_params=pltpu.CompilerParams(
            collective_id=0, has_side_effects=True, vmem_limit_bytes=34 * 1024 * 1024
        ),
    )(*(pltpu.with_memory_space_constraint(x, pltpu.HBM) for x in (routes.T, d_hidden, tokens, w_master)))
    hidden, update, new_master = pl.pallas_call(
        update_kernel,
        name="master_update",
        out_shape=(jax.ShapeDtypeStruct((slots, columns), bf16),)
        + (jax.ShapeDtypeStruct(w_master.shape, f32),) * 2,
        in_specs=[vmem] * 5,
        out_specs=(hbm, hbm, hbm),
        scratch_shapes=[
            pltpu.VMEM((2, rows, columns), f32),
            pltpu.VMEM((2, rows, columns), f32),
            dma((2, blocks)),
            dma((2, blocks)),
            dma((1,)),
        ],
        compiler_params=pltpu.CompilerParams(vmem_limit_bytes=30 * 1024 * 1024),
    )(inverse, colmax, grad, hidden, master)
    return (hidden, update, new_master)


def solution(mesh):
    in_specs = (P("row", None), P("row", None), P("row", None, "col"), P("row", "col"))
    out_specs = (P("row", "col"), P("row", None, "col"), P("row", None, "col"))
    return jax.shard_map(
        on_device, mesh=mesh, in_specs=in_specs, out_specs=out_specs, check_vma=False
    )
```
